32 devices in a mesh: groups: 2 (over x), tm: 8 (over z, y), tile: 2 (over core).
Axes of the slice: x: 2, y: 2, z: 4, core: 2. Of those that a mesh axis runs over, the one named last changes fastest.
Arguments:
- activations: bfloat16 [64, 24, 16, 16, 128], P(('groups', 'tm'), 'tile'), parts along dimension 0, may hold values from -240 to 240
- tile_ids: int32 [48], P(('groups', 'tile')), parts along dimension 0, may hold values from 0 to 15, as said below
- tile_counts: int32 [4], P(('groups', 'tile')), parts along dimension 0, may hold values from 0 to 12, as said below
- first_gain: float32 [128], replicated, may hold values from 0.25 to 1.75
- first_shift: float32 [128], replicated, may hold values from -3 to 3
- first_conv: bfloat16 [3, 3, 3, 128, 128], replicated, may hold values from -0.109375 to 0.109375
- first_down: bfloat16 [3, 3, 3, 128, 128], replicated, may hold values from -0.109375 to 0.109375
- second_gain: float32 [128], replicated, may hold values from 0.25 to 1.75
- second_shift: float32 [128], replicated, may hold values from -3 to 3
- second_conv: bfloat16 [3, 3, 3, 128, 256], replicated, may hold values from -0.109375 to 0.109375
- second_short: bfloat16 [128, 256], replicated, may hold values from -0.5 to 0.5
- second_down: bfloat16 [3, 3, 3, 256, 256], replicated, may hold values from -0.078125 to 0.078125
Outputs:
- latents: bfloat16 [16, 16, 4, 4, 256], P(('groups', 'tm'), 'tile'), parts along dimension 0
The draws below stay inside these ranges and needn't reach their ends.
There are 2 independent parts, one for each index of `groups`. The reference program is written for one: setup_inputs(seed, part) draws one part's arguments, and reference() takes and returns one part's arrays. A program takes and returns all parts, laid end to end along the dimension named above; an argument that names none is the same for every part. Nothing has to cross between parts.
Inputs may be any that keep to these rules, and one draw needn't show every extreme that they name: `tile_ids`: slot j belongs to tile device j // 12. The live slots of the two devices hold distinct tiles; tiles d * 8 to (d + 1) * 8 - 1 are owned by tile device d. Slots that are not live hold arbitrary tile numbers. The first tile_counts[d] slots of device d are live. One device holds exactly 12 live tiles, all 8 tiles of one owner among them; the other holds the remaining 4 tiles of the other owner or, for a clip of the lower resolution, none.
All inputs are finite; a program needn't handle non-finite values.
Results may differ from the reference program's by a relative error of at most 0.0066.
Values may be sent and summed in bfloat16 or wider, within the bound.
A program may use at most 64 MiB of HBM per device.

```python
import math
import jax
import jax.numpy as jnp
from jax import lax

C1 = 128
C2 = 256
GROUPS = 32
S = 16
OWN = 8
CAP = 12
TILES = 16
SLOTS = 24
FRAMES = 32


def draw_activations(key, part):
    subkeys = jax.random.split(jax.random.fold_in(key, 11), 5)
    full_shape = (FRAMES, SLOTS, S, S, C1)
    frame_pos = jnp.arange(FRAMES, dtype=jnp.float32) / (FRAMES - 1)
    frame_scale = jnp.exp(jax.random.uniform(subkeys[0], (FRAMES,), minval=math.log(0.3), maxval=math.log(3.0)))
    place_scale = jnp.exp(jax.random.uniform(subkeys[1], (S, S), minval=math.log(0.7), maxval=math.log(1.4)))
    channel_scale = jnp.exp(jax.random.uniform(subkeys[2], (C1,), minval=math.log(0.35), maxval=math.log(3.5)))
    offsets = jax.random.uniform(subkeys[3], (C1,), minval=-1.0, maxval=1.0)
    frame_scale = frame_scale * jnp.exp(frame_pos * math.log(3.0)) / 1.7
    noise_part = jnp.clip(jax.random.normal(subkeys[4], full_shape), -4.0, 4.0)
    scaled = noise_part * frame_scale[:, None, None, None, None] * place_scale[:, :, None] * channel_scale
    return (scaled + offsets * channel_scale).astype(jnp.bfloat16)


def tile_plan(key):
    subkeys = jax.random.split(jax.random.fold_in(key, 29), 6)
    heavy_dev = jax.random.randint(subkeys[0], (), 0, 2)
    low_res = jax.random.randint(subkeys[1], (), 0, 2)
    full_owner = jax.random.randint(subkeys[2], (), 0, 2)
    half_own = OWN // 2
    other_tiles = (1 - full_owner) * OWN + jax.random.permutation(subkeys[3], OWN)
    heavy_list = jnp.concatenate([full_owner * OWN + jnp.arange(OWN, dtype=jnp.int32), other_tiles[:half_own]])
    heavy_list = jax.random.permutation(subkeys[4], heavy_list)
    spare_ids = jax.random.randint(subkeys[5], (CAP - (OWN - half_own),), 0, TILES)
    light_list = jnp.concatenate([other_tiles[half_own:], spare_ids])
    light_count = (OWN - half_own) * (1 - low_res)
    tile_list = jnp.where(heavy_dev == 0, jnp.concatenate([heavy_list, light_list]), jnp.concatenate([light_list, heavy_list]))
    count_list = jnp.where(jnp.arange(2) == heavy_dev, CAP, light_count)
    return (tile_list.astype(jnp.int32), count_list.astype(jnp.int32))


def draw_tile_ids(key, part):
    return tile_plan(key)[0]


def draw_tile_counts(key, part):
    return tile_plan(key)[1]


def centred(rng, extent, deviation, reach, kind=jnp.bfloat16):
    return jnp.clip(deviation * jax.random.normal(rng, extent, jnp.float32), -reach, reach).astype(kind)


def setup_inputs(seed: int = 0, part: int = 0) -> dict:
    key_list = jax.random.split(jax.random.key(seed), 13)
    part_keys = jax.random.split(jax.random.fold_in(key_list[12], part), 13)
    activations = draw_activations(jax.random.fold_in(jax.random.fold_in(key_list[12], part), 71), part)
    tile_ids = draw_tile_ids(jax.random.fold_in(jax.random.fold_in(key_list[12], part), 71), part)
    tile_counts = draw_tile_counts(jax.random.fold_in(jax.random.fold_in(key_list[12], part), 71), part)
    first_gain = jnp.clip(1.0 + 0.15 * jax.random.normal(key_list[3], (C1,), jnp.float32), 0.25, 1.75)
    first_shift = centred(key_list[4], (C1,), 0.5, 3.0, jnp.float32)
    first_conv = centred(key_list[5], (3, 3, 3, C1, C1), (27 * C1) ** -0.5, 0.109375)
    first_down = centred(key_list[6], (3, 3, 3, C1, C1), (27 * C1) ** -0.5, 0.109375)
    second_gain = jnp.clip(1.0 + 0.15 * jax.random.normal(key_list[7], (C1,), jnp.float32), 0.25, 1.75)
    second_shift = centred(key_list[8], (C1,), 0.5, 3.0, jnp.float32)
    second_conv = centred(key_list[9], (3, 3, 3, C1, C2), (27 * C1) ** -0.5, 0.109375)
    second_short = centred(key_list[10], (C1, C2), C1 ** -0.5, 0.5)
    second_down = centred(key_list[11], (3, 3, 3, C2, C2), (27 * C2) ** -0.5, 0.078125)
    return dict(activations=activations, tile_ids=tile_ids, tile_counts=tile_counts, first_gain=first_gain, first_shift=first_shift, first_conv=first_conv, first_down=first_down, second_gain=second_gain, second_shift=second_shift, second_conv=second_conv, second_short=second_short, second_down=second_down)


epsilon = 1e-06

def causal_norm(inputs, norm_gain, norm_shift):
    frames = inputs.shape[0]
    tile_count = inputs.shape[1]
    tile_side = inputs.shape[2]
    per_group = inputs.shape[4] // GROUPS
    values = inputs.astype(jnp.float32).reshape(frames, tile_count, tile_side * tile_side, GROUPS, per_group)
    total_sum = jnp.cumsum(lax.optimization_barrier(jnp.sum(values, axis=(2, 4))), axis=0)
    total_square = jnp.cumsum(lax.optimization_barrier(jnp.sum(values * values, axis=(2, 4))), axis=0)
    counts = (jnp.arange(frames, dtype=jnp.float32) + 1.0) * float(tile_side * tile_side * per_group)
    mean_value = total_sum / counts[:, None, None]
    spread = total_square / counts[:, None, None] - mean_value * mean_value
    inverse = lax.rsqrt(spread + epsilon)
    normed = (values - mean_value[:, :, None, :, None]) * inverse[:, :, None, :, None]
    normed = normed.reshape(inputs.shape) * norm_gain + norm_shift
    return jax.nn.silu(normed).astype(jnp.bfloat16)

def causal_conv(inputs, kernel, stride):
    leading = jnp.concatenate([inputs[:1], inputs[:1]], axis=0)
    padded = jnp.concatenate([leading, inputs], axis=0)
    return lax.conv_general_dilated(padded, kernel, (stride, stride, stride), ((0, 0), (1, 1), (1, 1)), dimension_numbers=('DNHWC', 'DHWIO', 'DNHWC'), preferred_element_type=jnp.float32)

def reference(activations, tile_ids, tile_counts, first_gain, first_shift, first_conv, first_down, second_gain, second_shift, second_conv, second_short, second_down):
    slot_index = jnp.arange(SLOTS, dtype=jnp.int32)
    slot_live = slot_index % CAP < tile_counts[slot_index // CAP]
    tile_index = jnp.arange(TILES, dtype=jnp.int32)
    select_int = ((tile_ids[None, :] == tile_index[:, None]) & slot_live[None, :]).astype(jnp.int32)
    tile_live = lax.optimization_barrier(jnp.sum(select_int, axis=1)) > 0
    source_slot = lax.optimization_barrier(jnp.sum(select_int * slot_index[None, :], axis=1)).astype(jnp.int32)
    tile_data = jnp.take(activations, source_slot, axis=1)
    tile_data = jnp.where(tile_live[None, :, None, None, None], tile_data, jnp.zeros_like(tile_data))
    first_hidden = causal_norm(tile_data, first_gain, first_shift)
    first_sum = (tile_data.astype(jnp.float32) + causal_conv(first_hidden, first_conv, 1)).astype(jnp.bfloat16)
    first_level = causal_conv(first_sum, first_down, 2).astype(jnp.bfloat16)
    second_hidden = causal_norm(first_level, second_gain, second_shift)
    shortcut = jnp.dot(first_level.reshape(-1, first_level.shape[4]), second_short, preferred_element_type=jnp.float32)
    shortcut = shortcut.reshape(first_level.shape[:4] + (second_short.shape[1],))
    second_sum = (causal_conv(second_hidden, second_conv, 1) + shortcut).astype(jnp.bfloat16)
    encoded = causal_conv(second_sum, second_down, 2)
    return jnp.where(tile_live[None, :, None, None, None], encoded, jnp.zeros_like(encoded)).astype(jnp.bfloat16)
```

```python
import functools

import jax
import jax.numpy as jnp
import numpy as np
from jax import lax
from jax.experimental import pallas as pl
from jax.experimental.pallas import tpu as pltpu
from jax.sharding import PartitionSpec as P

GROUPS = 32
OWN = 8
MOVED = 4
EPS = 1e-06
F32 = jnp.float32
BF16 = jnp.bfloat16
SENT1 = jnp.bfloat16
SENT2 = jnp.bfloat16
MESH = pl.DeviceIdType.MESH
VMEM = pl.BlockSpec(memory_space=pltpu.VMEM)
SMEM = pl.BlockSpec(memory_space=pltpu.SMEM)
ANY = pl.BlockSpec(memory_space=pl.ANY)
LIMIT = 56 << 20


def silu_of_half(w):
    return w + w * jnp.tanh(w)


def shifted(v, side):
    rows = v.shape[0]
    col = lax.broadcasted_iota(jnp.int32, v.shape, 0) % side
    left = jnp.where(col == 0, 0.0, pltpu.roll(v, 1, axis=0))
    right = jnp.where(col == side - 1, 0.0, pltpu.roll(v, rows - 1, axis=0))
    return left, right


def plane_matrix():
    m = np.zeros((2, 2, OWN, 4, 4, OWN, 8, 8), np.float32)
    for yp in range(2):
        for xp in range(2):
            for t in range(OWN):
                for y in range(4):
                    for x in range(4):
                        m[yp, xp, t, y, x, t, 2 * y + yp, 2 * x + xp] = 1.0
    return m.reshape(OWN * 64, OWN * 64)


def main_kernel(
    n,
    per_frame,
    act_ref,
    ids_ref,
    count_ref,
    gain1_ref,
    shift1_ref,
    conv1_hbm,
    down1_hbm,
    gain2_ref,
    shift2_ref,
    conv2_hbm,
    short_hbm,
    down2_hbm,
    plane_hbm,
    out_ref,
    x,
    moved,
    info,
    rinfo,
    s_ref,
    conv2,
    conv2a,
    short,
    down2,
    down2a,
    plane,
    mine1,
    got1,
    mine2,
    got2,
    p1,
    p2,
    buf,
    ws,
    wn,
    wa,
    wd,
    wda,
    sf,
    lhs,
    own1,
    next1,
    part1,
    level,
    planes,
    blocks,
    ublocks,
    next2,
    part2,
    enc,
    renc,
    send1,
    recv1,
    send2,
    recv2,
    psend,
    precv,
    sems,
    local,
):
    me = lax.axis_index("tm")
    partner = 1 - lax.axis_index("tile")
    cap = act_ref.shape[1]
    used = [0]

    def copy_in(src, dst):
        c = pltpu.make_async_copy(src, dst, local.at[used[0]])
        used[0] += 1
        return c

    half = OWN - MOVED
    fetch = [
        copy_in(act_ref.at[:, 0:half], x.at[:, 0:half]),
        copy_in(act_ref.at[:, half:OWN], x.at[:, half:OWN]),
    ]
    for c in fetch:
        c.start()
    barrier = pltpu.get_barrier_semaphore()
    for k in range(1, n):
        pl.semaphore_signal(barrier, inc=1, device_id={"tm": lax.rem(me + k, n)}, device_id_type=MESH)
    pl.semaphore_signal(barrier, inc=1, device_id={"tile": partner}, device_id_type=MESH)

    lane = lax.broadcasted_iota(jnp.int32, (1, 128), 1)
    count = count_ref[0]
    heavy = jnp.full((1, 128), count, jnp.int32) == cap

    def row_ids(slots):
        v = jnp.full((1, 128), -1, jnp.int32)
        for j, slot in enumerate(slots):
            v = jnp.where(lane // 16 == j, jnp.where(slot < count, ids_ref[slot], -1), v)
        return v

    info[0:1] = row_ids(range(OWN))
    info[1:2] = row_ids(list(range(half)) + list(range(OWN, OWN + MOVED)))
    info[2:8] = jnp.full((6, 128), count, jnp.int32)

    def remote(src, dst, send_sem, recv_sem, target):
        return pltpu.make_async_remote_copy(
            src_ref=src, dst_ref=dst, send_sem=send_sem, recv_sem=recv_sem, device_id=target, device_id_type=MESH
        )

    def swap(src, dst, i):
        return remote(src, dst, sems.at[2 * i], sems.at[2 * i + 1], {"tile": partner})

    def share(mine, got, send_sem, recv_sem):
        copies = []
        for k in range(1, n):
            c = remote(mine, got.at[k], send_sem.at[k], recv_sem.at[k], {"tm": lax.rem(me + k, n)})
            c.start()
            copies.append(c)
        return copies

    def norms(sums, copies, got, gain, shift, size, out):
        frames = len(sums)
        run = jnp.zeros_like(sums[0])
        for k in range(n - 1, 0, -1):
            copies[k - 1].wait()
            run = run + jnp.where(k <= me, got[k], 0.0)
        rows = []
        for f in range(frames):
            run = run + sums[f]
            rows.append(run)
        ri = lax.broadcasted_iota(jnp.int32, (128, 128), 0) // (128 // GROUPS)
        ci = lax.broadcasted_iota(jnp.int32, (128, 128), 1) // (128 // GROUPS)
        same = jnp.where(ri == ci, 1.0, 0.0).astype(F32)
        grouped = jnp.dot(
            jnp.concatenate(rows, axis=0), same, precision=lax.Precision.HIGHEST, preferred_element_type=F32
        )
        start = (me * frames).astype(F32)
        for i in range(frames):
            inv_count = jnp.full((1, 128), 1.0, F32) / (jnp.zeros((1, 128), F32) + (start + float(i + 1)) * size)
            g = grouped[i * 2 * OWN : (i + 1) * 2 * OWN]
            m = g[0:OWN] * inv_count
            var = g[OWN : 2 * OWN] * inv_count - m * m
            scale = lax.rsqrt(var + EPS) * gain[...]
            out[i, 0] = 0.5 * scale
            out[i, 1] = 0.5 * (shift[...] - m * scale)

    zero = jnp.zeros((384, 128), BF16)
    for b in range(3):
        ws[b, 384:768, 0:128] = zero
        wa[b, 384:768, 0:128] = zero
        wn[b, 0:384, 128:256] = zero
        wd[b, 384:768, 0:128] = zero
        wda[b, 384:768, 0:128] = zero
    edge = jnp.zeros((16, 768), BF16)
    for z in range(2):
        for p in range(2):
            for r in (0, 272, 544):
                buf[z, p, r : r + 16] = edge

    pl.semaphore_wait(barrier, n)
    move_copies = [swap(act_ref.at[:, OWN + i], moved.at[:, i], 2 + i) for i in range(MOVED)]
    for c in move_copies:
        c.start()
    info_copy = swap(info, rinfo, 0)
    info_copy.start()

    top, low = slice(0, 384), slice(384, 768)
    first, second = slice(0, 128), slice(128, 256)
    early = [
        copy_in(h.at[a], w.at[:, r, c])
        for h, a, w, r, c in (
            (conv1_hbm, 0, wn, top, first),
            (conv1_hbm, 1, wn, low, first),
            (conv1_hbm, 0, wn, low, second),
            (conv1_hbm, 2, ws, top, first),
            (conv1_hbm, 1, ws, top, second),
            (conv1_hbm, 2, ws, low, second),
            (conv1_hbm, 2, wa, top, first),
            (conv1_hbm, 1, wa, top, second),
            (conv1_hbm, 2, wa, low, second),
            (down1_hbm, 2, wd, top, first),
            (down1_hbm, 0, wd, top, second),
            (down1_hbm, 1, wd, low, second),
            (down1_hbm, 2, wda, top, first),
            (down1_hbm, 0, wda, top, second),
            (down1_hbm, 1, wda, low, second),
        )
    ]
    late = [
        copy_in(a, b)
        for a, b in (
            (plane_hbm, plane),
            (conv2_hbm, conv2),
            (conv2_hbm.at[2], conv2a.at[0]),
            (conv2_hbm.at[1], conv2a.at[1]),
            (short_hbm, short),
            (down2_hbm, down2),
            (down2_hbm.at[2], down2a),
        )
    ]

    def add_up(f, j, v):
        s_ref[f, pl.ds(j, 1), :] = jnp.sum(v, axis=0, keepdims=True)
        s_ref[f, pl.ds(OWN + j, 1), :] = jnp.sum(v * v, axis=0, keepdims=True)

    fetch[0].wait()

    def count_own(j, _):
        for f in range(4):
            add_up(f, j, x[f, j].astype(F32).reshape(256, 128))
        return 0

    lax.fori_loop(0, half, count_own, 0)
    fetch[1].wait()
    for c in early:
        c.start()
    for i in range(MOVED):
        move_copies[i].wait()

    def count_moved(i, _):
        j = half + i
        for f in range(4):
            a = x[f, j].astype(F32).reshape(256, 128)
            v = jnp.where(heavy, a, moved[f, i].astype(F32).reshape(256, 128))
            x[f, j] = v.astype(BF16).reshape(x.shape[2:])
            add_up(f, j, v)
        return 0

    lax.fori_loop(0, MOVED, count_moved, 0)
    sums1 = [s_ref[f] for f in range(4)]
    mine1[...] = sums1[0] + sums1[1] + sums1[2] + sums1[3]
    copies1 = share(mine1, got1, send1, recv1)
    for c in late:
        c.start()
    for c in early:
        c.wait()

    def sum_of(*refs):
        total = refs[0].astype(F32)
        for r in refs[1:]:
            total = total + r.astype(F32)
        return total.astype(BF16)

    @pl.when(me == 0)
    def _():
        for b in range(3):
            k0, k1, k2 = wn[b, top, first], ws[b, top, second], ws[b, top, first]
            wa[b, top, first] = sum_of(k0, k1, k2)
            wa[b, top, second] = sum_of(k0, k1)
            wda[b, top, first] = sum_of(wd[b, top, first], wd[b, top, second], wd[b, low, second])

    norms(sums1, copies1, got1, gain1_ref, shift1_ref, per_frame, p1)

    def prep(i, z):
        for t in range(2):
            j = 2 * i + t
            rows = slice(16 + t * 272, 272 + t * 272)
            for q in range(4):
                v = x[q, j].astype(F32).reshape(256, 128)
                h = silu_of_half(v * p1[q, 0, pl.ds(j, 1), :] + p1[q, 1, pl.ds(j, 1), :])
                left, right = shifted(h, 16)
                k = (q % 2) * 384
                buf[z, q // 2, rows, k : k + 128] = left.astype(BF16)
                buf[z, q // 2, rows, k + 128 : k + 256] = h.astype(BF16)
                buf[z, q // 2, rows, k + 256 : k + 384] = right.astype(BF16)

    def multiply(i, z):
        def pair(p, b):
            r = b * 16
            return jnp.concatenate([buf[z, p, r : r + 256, :], buf[z, p, r + 272 : r + 528, :]], axis=0)

        def conv(terms):
            acc = jnp.zeros((512, 256), F32)
            for p, w in terms:
                for b in range(3):
                    acc = acc + jnp.dot(pair(p, b), w[b], preferred_element_type=F32)
            return acc

        col = lax.broadcasted_iota(jnp.int32, (256, 128), 0) % 8

        def down(which, acc, frame, w):
            for e in range(2):
                for t in range(2):
                    v = acc[t * 256 : t * 256 + 256, e * 128 : e * 128 + 128]
                    if frame is not None:
                        v = v + x[frame + e, 2 * i + t].astype(F32).reshape(256, 128)
                    sf[z, which, e, t * 256 : t * 256 + 256] = v
            for e in range(2):
                even = sf[z, which, e, pl.ds(0, 256, stride=2), :]
                odd = sf[z, which, e, pl.ds(1, 256, stride=2), :]
                prev = jnp.where(col == 0, 0.0, pltpu.roll(odd, 1, axis=0))
                for c, v in enumerate((prev, even, odd)):
                    v = v.reshape(2, 8, 2, 8, 128)
                    up_rows, low_rows = v[:, :, 0], v[:, :, 1]
                    above = jnp.concatenate([jnp.zeros((2, 1, 8, 128), F32), low_rows[:, :7]], axis=1)
                    k = e * 384 + c * 128
                    for b, u in enumerate((above, up_rows, low_rows)):
                        lhs[z, which, b, :, k : k + 128] = u.reshape(128, 128).astype(BF16)
            out = jnp.zeros((128, 256), F32)
            for b in range(3):
                out = out + jnp.dot(lhs[z, which, b], w[b], preferred_element_type=F32)
            return out

        out_c = down(2, conv(((1, wn),)), None, wd)
        out_b = down(1, conv(((1, ws), (0, wn))), 2, wd)
        next1[i, 0] = (out_b[:, second] + out_c[:, first]).astype(SENT1)
        next1[i, 1] = out_c[:, second].astype(SENT1)
        out_a = down(0, conv(((0, wa),)), 0, wda)
        own1[i, 0] = out_a[:, first]
        own1[i, 1] = out_a[:, second] + out_b[:, first]

    def part_copy(i):
        return remote(next1.at[i], part1.at[i], psend.at[i], precv.at[i], {"tm": lax.rem(me + 1, n)})

    pairs = OWN // 2

    def step(i, _):
        prep(2 * i + 1, 1)
        multiply(2 * i, 0)
        prep(jnp.minimum(2 * i + 2, pairs - 1), 0)
        multiply(2 * i + 1, 1)
        part_copy(2 * i).start()
        part_copy(2 * i + 1).start()
        return 0

    prep(0, 0)
    lax.fori_loop(0, pairs // 2, step, 0)
    for i in range(pairs):
        part_copy(i).wait()
        for f in range(2):
            v = own1[i, f] + jnp.where(me > 0, part1[i, f].astype(F32), 0.0)
            level[i * 128 : i * 128 + 128, f * 128 : f * 128 + 128] = v.astype(BF16)
    sums2 = []
    for f in range(2):
        v = level[:, f * 128 : f * 128 + 128].astype(F32).reshape(OWN, 64, 128)
        sums2.append(jnp.concatenate([jnp.sum(v, axis=1), jnp.sum(v * v, axis=1)], axis=0))
    mine2[...] = sums2[0] + sums2[1]
    copies2 = share(mine2, got2, send2, recv2)
    for c in late:
        c.wait()
    planes[...] = jnp.dot(plane[...], level[...], preferred_element_type=F32).astype(BF16)

    @pl.when(me == 0)
    def _():
        conv2a[0] = sum_of(conv2[0], conv2[1], conv2[2])
        conv2a[1] = sum_of(conv2[0], conv2[1])
        for i in range(9):
            down2a[i] = sum_of(down2[0, i], down2[1, i], down2[2, i])

    norms(sums2, copies2, got2, gain2_ref, shift2_ref, per_frame / 4, p2)

    row = lax.broadcasted_iota(jnp.int32, (128, 128), 0)

    def back_y(v, row):
        return jnp.where(row % 16 < 4, 0.0, pltpu.roll(v, 4, axis=0))

    def back_x(v, row):
        return jnp.where(row % 4 < 1, 0.0, pltpu.roll(v, 1, axis=0))

    def on_y(v, row):
        return jnp.where(row % 16 >= 12, 0.0, pltpu.roll(v, 124, axis=0))

    def on_x(v, row):
        return jnp.where(row % 4 >= 3, 0.0, pltpu.roll(v, 127, axis=0))

    for f in range(2):
        scale = p2[f, 0].reshape(OWN, 1, 128)
        bias = p2[f, 1].reshape(OWN, 1, 128)
        for yp in range(2):
            for xp in range(2):
                q = yp * 2 + xp
                v = planes[q * 128 : q * 128 + 128, f * 128 : f * 128 + 128].astype(F32)
                h = silu_of_half(v.reshape(OWN, 16, 128) * scale + bias).reshape(128, 128)
                hy = (back_y if yp else on_y)(h, row)
                move_x = back_x if xp else on_x
                for s, u in enumerate((h, move_x(h, row), hy, move_x(hy, row))):
                    blocks[f, q * 4 + s] = u.astype(BF16)

    taps = (((1, 1), (0, 0), (1, 0)), ((0, 0), (1, 0), (0, 1)))

    def gathered(f):
        rows = []
        for yp in range(2):
            for xp in range(2):
                cells = []
                for b in range(3):
                    for c in range(3):
                        (py, sy), (px, sx) = taps[yp][b], taps[xp][c]
                        cells.append(blocks[f, (py * 2 + px) * 4 + sy * 2 + sx])
                rows.append(jnp.concatenate(cells, axis=1))
        return jnp.concatenate(rows, axis=0)

    row2 = lax.broadcasted_iota(jnp.int32, (128, 256), 0)

    def spread(which, acc):
        u = [acc[q * 128 : q * 128 + 128] for q in range(4)]
        u1x, u3x, u2y, u3y = back_x(u[1], row2), back_x(u[3], row2), back_y(u[2], row2), back_y(u[3], row2)
        u3yx = back_x(u3y, row2)
        for i, v in enumerate((u3yx, u2y, u3y, u1x, u[0], u[1], u3x, u[2], u[3])):
            ublocks[which, i] = v.astype(BF16)

    def dot(a, b):
        return jnp.dot(a, b, preferred_element_type=F32)

    spread(3, dot(gathered(1), conv2[0]))
    spread(2, dot(gathered(0), conv2[0]) + dot(gathered(1), conv2[1]))

    def down_sum(terms):
        acc = jnp.zeros((128, 256), F32)
        for which, w in terms:
            for i in range(9):
                acc = acc + dot(ublocks[which, i], w[i])
        return acc

    next2[1] = down_sum(((2, down2.at[0]), (3, down2.at[1]))).astype(SENT2)
    skip_copy = remote(next2.at[1], part2.at[1], sems.at[12], sems.at[13], {"tm": lax.rem(me + 2, n)})
    skip_copy.start()
    spread(1, dot(gathered(0), conv2a[1]) + dot(gathered(1), conv2[2]) + dot(planes[:, second], short[...]))
    spread(0, dot(gathered(0), conv2a[0]) + dot(planes[:, first], short[...]))
    next2[0] = down_sum(((0, down2.at[0]), (1, down2.at[1]), (2, down2.at[2]))).astype(SENT2)
    next_copy = remote(next2.at[0], part2.at[0], sems.at[14], sems.at[15], {"tm": lax.rem(me + 1, n)})
    next_copy.start()
    own = down_sum(((0, down2a),))
    info_copy.wait()
    low_lane = lane < half * 16
    its_heavy = rinfo[2:3, :] == cap
    my_ids = jnp.where(low_lane | heavy, info[0:1, :], rinfo[1:2, :])
    its_ids = jnp.where(low_lane | its_heavy, rinfo[0:1, :], info[1:2, :])
    wanted = lax.axis_index("tile") * OWN + row // 16
    cell = row % 16 == lax.broadcasted_iota(jnp.int32, (128, 128), 1) % 16
    mine = jnp.where((wanted == my_ids) & cell, 1.0, 0.0).astype(BF16)
    its = jnp.where((wanted == its_ids) & cell, 1.0, 0.0).astype(BF16)
    skip_copy.wait()
    own = own + jnp.where(me > 1, part2[1].astype(F32), 0.0)
    next_copy.wait()
    enc[...] = (own + jnp.where(me > 0, part2[0].astype(F32), 0.0)).astype(BF16)
    enc_copy = swap(enc, renc, 1)
    enc_copy.start()
    kept = dot(mine, enc[...])
    enc_copy.wait()
    out_ref[...] = (kept + dot(its, renc[...])).astype(BF16)


def encode(acts, ids, counts, params, n):
    (
        first_gain,
        first_shift,
        first_conv,
        first_down,
        second_gain,
        second_shift,
        second_conv,
        second_short,
        second_down,
    ) = params
    cells = acts.shape[2:]
    rows = OWN * 64
    vm = pltpu.VMEM
    line = lambda v: v.reshape(1, 128)
    return pl.pallas_call(
        functools.partial(main_kernel, n, float(cells[0] * cells[1] * (cells[2] // GROUPS))),
        out_shape=jax.ShapeDtypeStruct((OWN * 16, 256), BF16),
        in_specs=[ANY, SMEM, SMEM, VMEM, VMEM, ANY, ANY, VMEM, VMEM, ANY, ANY, ANY, ANY],
        out_specs=VMEM,
        scratch_shapes=[
            vm((4, OWN) + cells, BF16),
            vm((4, MOVED) + cells, BF16),
            vm((8, 128), jnp.int32),
            vm((8, 128), jnp.int32),
            vm((4, 2 * OWN, 128), F32),
            vm((3, 1152, 256), BF16),
            vm((2, 1152, 256), BF16),
            vm((128, 256), BF16),
            vm((3, 9, 256, 256), BF16),
            vm((9, 256, 256), BF16),
            vm((rows, rows), BF16),
            vm((2 * OWN, 128), F32),
            vm((n, 2 * OWN, 128), F32),
            vm((2 * OWN, 128), F32),
            vm((n, 2 * OWN, 128), F32),
            vm((4, 2, OWN, 128), F32),
            vm((2, 2, OWN, 128), F32),
            vm((2, 2, 560, 768), BF16),
            vm((3, 768, 256), BF16),
            vm((3, 768, 256), BF16),
            vm((3, 768, 256), BF16),
            vm((3, 768, 256), BF16),
            vm((3, 768, 256), BF16),
            vm((2, 3, 2, 512, 128), F32),
            vm((2, 3, 3, 128, 768), BF16),
            vm((OWN // 2, 2, 128, 128), F32),
            vm((OWN // 2, 2, 128, 128), SENT1),
            vm((OWN // 2, 2, 128, 128), SENT1),
            vm((rows, 256), BF16),
            vm((rows, 256), BF16),
            vm((2, 16, 128, 128), BF16),
            vm((4, 9, 128, 256), BF16),
            vm((2, OWN * 16, 256), SENT2),
            vm((2, OWN * 16, 256), SENT2),
            vm((OWN * 16, 256), BF16),
            vm((OWN * 16, 256), BF16),
            pltpu.SemaphoreType.DMA((n,)),
            pltpu.SemaphoreType.DMA((n,)),
            pltpu.SemaphoreType.DMA((n,)),
            pltpu.SemaphoreType.DMA((n,)),
            pltpu.SemaphoreType.DMA((OWN // 2,)),
            pltpu.SemaphoreType.DMA((OWN // 2,)),
            pltpu.SemaphoreType.DMA((16,)),
            pltpu.SemaphoreType.DMA((24,)),
        ],
        name="encode",
        compiler_params=pltpu.CompilerParams(collective_id=0, has_side_effects=True, vmem_limit_bytes=LIMIT),
    )(
        acts,
        ids,
        counts,
        line(first_gain),
        line(first_shift),
        first_conv.reshape(3, 3, 384, 128),
        first_down.reshape(3, 3, 384, 128),
        line(second_gain),
        line(second_shift),
        second_conv.reshape(3, 1152, 256),
        second_short,
        second_down.reshape(3, 9, 256, 256),
        jnp.asarray(plane_matrix(), BF16),
    )


def body(activations, tile_ids, tile_counts, *params):
    n = lax.axis_size("tm")
    latents = encode(activations, tile_ids, tile_counts, params, n)
    return latents.reshape(1, OWN, 4, 4, 256)


def solution(mesh):
    placed = (
        P(("groups", "tm"), "tile", None, None, None),
        P(("groups", "tile")),
        P(("groups", "tile")),
    ) + (P(),) * 9
    return jax.shard_map(
        body,
        mesh=mesh,
        in_specs=placed,
        out_specs=P(("groups", "tm"), "tile", None, None, None),
        check_vma=False,
    )
```

```python
import functools

import jax
import jax.numpy as jnp
import numpy as np
from jax import lax
from jax.experimental import pallas as pl
from jax.experimental.pallas import tpu as pltpu
from jax.sharding import PartitionSpec as P

GROUPS = 32
OWN = 8
MOVED = 4
EPS = 1e-06
F32 = jnp.float32
BF16 = jnp.bfloat16
SENT1 = jnp.bfloat16
SENT2 = jnp.bfloat16
MESH = pl.DeviceIdType.MESH
VMEM = pl.BlockSpec(memory_space=pltpu.VMEM)
SMEM = pl.BlockSpec(memory_space=pltpu.SMEM)
ANY = pl.BlockSpec(memory_space=pl.ANY)
LIMIT = 56 << 20


def silu_of_half(w):
    return w + w * jnp.tanh(w)


def shifted(v, side):
    rows = v.shape[0]
    col = lax.broadcasted_iota(jnp.int32, v.shape, 0) % side
    left = jnp.where(col == 0, 0.0, pltpu.roll(v, 1, axis=0))
    right = jnp.where(col == side - 1, 0.0, pltpu.roll(v, rows - 1, axis=0))
    return left, right


def plane_matrix():
    m = np.zeros((2, 2, OWN, 4, 4, OWN, 8, 8), np.float32)
    for yp in range(2):
        for xp in range(2):
            for t in range(OWN):
                for y in range(4):
                    for x in range(4):
                        m[yp, xp, t, y, x, t, 2 * y + yp, 2 * x + xp] = 1.0
    return m.reshape(OWN * 64, OWN * 64)


def main_kernel(
    n,
    per_frame,
    act_ref,
    ids_ref,
    count_ref,
    gain1_ref,
    shift1_ref,
    conv1_hbm,
    down1_hbm,
    gain2_ref,
    shift2_ref,
    conv2_hbm,
    short_hbm,
    down2_hbm,
    plane_hbm,
    out_ref,
    x,
    moved,
    info,
    rinfo,
    s_ref,
    conv2,
    conv2a,
    short,
    down2,
    down2a,
    plane,
    mine1,
    got1,
    mine2,
    got2,
    p1,
    p2,
    bufe,
    bufo,
    ws,
    wn,
    wa,
    wd,
    wda,
    sf,
    lhs,
    outd,
    next1,
    part1,
    level,
    planes,
    blocks,
    ublocks,
    next2,
    part2,
    enc,
    renc,
    send1,
    recv1,
    send2,
    recv2,
    psend,
    precv,
    sems,
    local,
):
    me = lax.axis_index("tm")
    partner = 1 - lax.axis_index("tile")
    cap = act_ref.shape[1]
    used = [0]

    def copy_in(src, dst):
        c = pltpu.make_async_copy(src, dst, local.at[used[0]])
        used[0] += 1
        return c

    half = OWN - MOVED
    fetch = [
        copy_in(act_ref.at[:, 0:half], x.at[:, 0:half]),
        copy_in(act_ref.at[:, half:OWN], x.at[:, half:OWN]),
    ]
    for c in fetch:
        c.start()
    barrier = pltpu.get_barrier_semaphore()
    for k in range(1, n):
        pl.semaphore_signal(barrier, inc=1, device_id={"tm": lax.rem(me + k, n)}, device_id_type=MESH)
    pl.semaphore_signal(barrier, inc=1, device_id={"tile": partner}, device_id_type=MESH)

    lane = lax.broadcasted_iota(jnp.int32, (1, 128), 1)
    count = count_ref[0]
    heavy = jnp.full((1, 128), count, jnp.int32) == cap

    def row_ids(slots):
        v = jnp.full((1, 128), -1, jnp.int32)
        for j, slot in enumerate(slots):
            v = jnp.where(lane // 16 == j, jnp.where(slot < count, ids_ref[slot], -1), v)
        return v

    info[0:1] = row_ids(range(OWN))
    info[1:2] = row_ids(list(range(half)) + list(range(OWN, OWN + MOVED)))
    info[2:8] = jnp.full((6, 128), count, jnp.int32)

    def remote(src, dst, send_sem, recv_sem, target):
        return pltpu.make_async_remote_copy(
            src_ref=src, dst_ref=dst, send_sem=send_sem, recv_sem=recv_sem, device_id=target, device_id_type=MESH
        )

    def swap(src, dst, i):
        return remote(src, dst, sems.at[2 * i], sems.at[2 * i + 1], {"tile": partner})

    def share(mine, got, send_sem, recv_sem):
        copies = []
        for k in range(1, n):
            c = remote(mine, got.at[k], send_sem.at[k], recv_sem.at[k], {"tm": lax.rem(me + k, n)})
            c.start()
            copies.append(c)
        return copies

    def norms(sums, copies, got, gain, shift, size, out):
        frames = len(sums)
        run = jnp.zeros_like(sums[0])
        for k in range(n - 1, 0, -1):
            copies[k - 1].wait()
            run = run + jnp.where(k <= me, got[k], 0.0)
        rows = []
        for f in range(frames):
            run = run + sums[f]
            rows.append(run)
        ri = lax.broadcasted_iota(jnp.int32, (128, 128), 0) // (128 // GROUPS)
        ci = lax.broadcasted_iota(jnp.int32, (128, 128), 1) // (128 // GROUPS)
        same = jnp.where(ri == ci, 1.0, 0.0).astype(F32)
        grouped = jnp.dot(
            jnp.concatenate(rows, axis=0), same, precision=lax.Precision.HIGHEST, preferred_element_type=F32
        )
        start = (me * frames).astype(F32)
        for i in range(frames):
            inv_count = jnp.full((1, 128), 1.0, F32) / (jnp.zeros((1, 128), F32) + (start + float(i + 1)) * size)
            g = grouped[i * 2 * OWN : (i + 1) * 2 * OWN]
            m = g[0:OWN] * inv_count
            var = g[OWN : 2 * OWN] * inv_count - m * m
            scale = lax.rsqrt(var + EPS) * gain[...]
            out[i, 0] = 0.5 * scale
            out[i, 1] = 0.5 * (shift[...] - m * scale)

    zero = jnp.zeros((384, 128), BF16)
    for b in range(3):
        ws[b, 384:768, 0:128] = zero
        wa[b, 384:768, 0:128] = zero
        wn[b, 0:384, 128:256] = zero
        wd[b, 384:768, 0:128] = zero
        wda[b, 384:768, 0:128] = zero
    edge = jnp.zeros((16, 768), BF16)
    for tiles in (bufe, bufo):
        for i in range(2):
            for p in range(2):
                for r in (0, 272, 544):
                    tiles[i, p, r : r + 16] = edge

    pl.semaphore_wait(barrier, n)
    move_copies = [swap(act_ref.at[:, OWN + i], moved.at[:, i], 2 + i) for i in range(MOVED)]
    for c in move_copies:
        c.start()
    info_copy = swap(info, rinfo, 0)
    info_copy.start()

    top, low = slice(0, 384), slice(384, 768)
    first, second = slice(0, 128), slice(128, 256)
    early = [
        copy_in(h.at[a], w.at[:, r, c])
        for h, a, w, r, c in (
            (conv1_hbm, 0, wn, top, first),
            (conv1_hbm, 1, wn, low, first),
            (conv1_hbm, 0, wn, low, second),
            (conv1_hbm, 2, ws, top, first),
            (conv1_hbm, 1, ws, top, second),
            (conv1_hbm, 2, ws, low, second),
            (conv1_hbm, 2, wa, top, first),
            (conv1_hbm, 1, wa, top, second),
            (conv1_hbm, 2, wa, low, second),
            (down1_hbm, 2, wd, top, first),
            (down1_hbm, 0, wd, top, second),
            (down1_hbm, 1, wd, low, second),
            (down1_hbm, 2, wda, top, first),
            (down1_hbm, 0, wda, top, second),
            (down1_hbm, 1, wda, low, second),
        )
    ]
    late = [
        copy_in(a, b)
        for a, b in (
            (plane_hbm, plane),
            (conv2_hbm, conv2),
            (conv2_hbm.at[2], conv2a.at[0]),
            (conv2_hbm.at[1], conv2a.at[1]),
            (short_hbm, short),
            (down2_hbm, down2),
            (down2_hbm.at[2], down2a),
        )
    ]

    def add_up(f, j, v):
        s_ref[f, pl.ds(j, 1), :] = jnp.sum(v, axis=0, keepdims=True)
        s_ref[f, pl.ds(OWN + j, 1), :] = jnp.sum(v * v, axis=0, keepdims=True)

    fetch[0].wait()

    def count_own(j, _):
        for f in range(4):
            add_up(f, j, x[f, j].astype(F32).reshape(256, 128))
        return 0

    lax.fori_loop(0, half, count_own, 0)
    fetch[1].wait()
    for c in early:
        c.start()
    for i in range(MOVED):
        move_copies[i].wait()

    def count_moved(i, _):
        j = half + i
        for f in range(4):
            a = x[f, j].astype(F32).reshape(256, 128)
            v = jnp.where(heavy, a, moved[f, i].astype(F32).reshape(256, 128))
            x[f, j] = v.astype(BF16).reshape(x.shape[2:])
            add_up(f, j, v)
        return 0

    lax.fori_loop(0, MOVED, count_moved, 0)
    sums1 = [s_ref[f] for f in range(4)]
    mine1[...] = sums1[0] + sums1[1] + sums1[2] + sums1[3]
    copies1 = share(mine1, got1, send1, recv1)
    for c in late:
        c.start()
    for c in early:
        c.wait()

    def sum_of(*refs):
        total = refs[0].astype(F32)
        for r in refs[1:]:
            total = total + r.astype(F32)
        return total.astype(BF16)

    @pl.when(me == 0)
    def _():
        for b in range(3):
            k0, k1, k2 = wn[b, top, first], ws[b, top, second], ws[b, top, first]
            wa[b, top, first] = sum_of(k0, k1, k2)
            wa[b, top, second] = sum_of(k0, k1)
            wda[b, top, first] = sum_of(wd[b, top, first], wd[b, top, second], wd[b, low, second])

    norms(sums1, copies1, got1, gain1_ref, shift1_ref, per_frame, p1)

    def prep(i, tiles):
        for t in range(2):
            j = 2 * i + t
            rows = slice(16 + t * 272, 272 + t * 272)
            for q in range(4):
                v = x[q, j].astype(F32).reshape(256, 128)
                h = silu_of_half(v * p1[q, 0, pl.ds(j, 1), :] + p1[q, 1, pl.ds(j, 1), :])
                left, right = shifted(h, 16)
                k = (q % 2) * 384
                tiles[q // 2, rows, k : k + 128] = left.astype(BF16)
                tiles[q // 2, rows, k + 128 : k + 256] = h.astype(BF16)
                tiles[q // 2, rows, k + 256 : k + 384] = right.astype(BF16)

    def conv(tiles, terms):
        acc = jnp.zeros((512, 256), F32)
        for p, w in terms:
            for b in range(3):
                r = b * 16
                pair = jnp.concatenate([tiles[p, r : r + 256, :], tiles[p, r + 272 : r + 528, :]], axis=0)
                acc = acc + jnp.dot(pair, w[b], preferred_element_type=F32)
        return acc

    def build(i, z, which, acc, frame):
        col = lax.broadcasted_iota(jnp.int32, (256, 128), 0) % 8
        rows = pl.ds(pl.multiple_of(i * 128, 128), 128)
        for e in range(2):
            for t in range(2):
                v = acc[t * 256 : t * 256 + 256, e * 128 : e * 128 + 128]
                if frame is not None:
                    v = v + x[frame + e, 2 * i + t].astype(F32).reshape(256, 128)
                sf[z, which, e, t * 256 : t * 256 + 256] = v
        for e in range(2):
            even = sf[z, which, e, pl.ds(0, 256, stride=2), :]
            odd = sf[z, which, e, pl.ds(1, 256, stride=2), :]
            prev = jnp.where(col == 0, 0.0, pltpu.roll(odd, 1, axis=0))
            for c, v in enumerate((prev, even, odd)):
                v = v.reshape(2, 8, 2, 8, 128)
                up_rows, low_rows = v[:, :, 0], v[:, :, 1]
                above = jnp.concatenate([jnp.zeros((2, 1, 8, 128), F32), low_rows[:, :7]], axis=1)
                k = e * 384 + c * 128
                for b, u in enumerate((above, up_rows, low_rows)):
                    lhs[which, b, rows, k : k + 128] = u.reshape(128, 128).astype(BF16)

    def down(which, rows, w):
        out = jnp.dot(lhs[which, 0, rows, :], w[0], preferred_element_type=F32)
        for b in range(1, 3):
            out = out + jnp.dot(lhs[which, b, rows, :], w[b], preferred_element_type=F32)
        outd[which, rows, :] = out

    pairs = OWN // 2

    def part_copy(i):
        return remote(next1.at[i], part1.at[i], psend.at[i], precv.at[i], {"tm": lax.rem(me + 1, n)})

    def step(i, _):
        def onward(pair, z, tiles):
            build(pair, z, 2, conv(tiles, ((1, wn),)), None)
            build(pair, z, 1, conv(tiles, ((1, ws), (0, wn))), 2)

        prep(2 * i + 1, bufo.at[i])
        onward(2 * i, 0, bufe.at[i])
        prep(jnp.minimum(2 * i + 2, pairs - 1), bufe.at[i + 1])
        onward(2 * i + 1, 1, bufo.at[i])
        rows = pl.ds(pl.multiple_of(i * 256, 256), 256)

        def each(k, _):
            down(1 + k, rows, wd)
            return 0

        lax.fori_loop(0, 2, each, 0)
        next1[i, 0] = (outd[1, rows, second] + outd[2, rows, first]).astype(SENT1)
        next1[i, 1] = outd[2, rows, second].astype(SENT1)
        part_copy(i).start()
        return 0

    prep(0, bufe.at[0])
    lax.fori_loop(0, 2, step, 0)

    def own_step(i, _):
        build(2 * i, 0, 0, conv(bufe.at[i], ((0, wa),)), 0)
        build(2 * i + 1, 1, 0, conv(bufo.at[i], ((0, wa),)), 0)
        return 0

    lax.fori_loop(0, 2, own_step, 0)
    down(0, slice(0, OWN * 64), wda)
    for i in range(2):
        part_copy(i).wait()
        rows = slice(i * 256, i * 256 + 256)
        for f in range(2):
            v = outd[0, rows, f * 128 : f * 128 + 128]
            if f == 1:
                v = v + outd[1, rows, first]
            v = v + jnp.where(me > 0, part1[i, f].astype(F32), 0.0)
            level[rows, f * 128 : f * 128 + 128] = v.astype(BF16)
    sums2 = []
    for f in range(2):
        v = level[:, f * 128 : f * 128 + 128].astype(F32).reshape(OWN, 64, 128)
        sums2.append(jnp.concatenate([jnp.sum(v, axis=1), jnp.sum(v * v, axis=1)], axis=0))
    mine2[...] = sums2[0] + sums2[1]
    copies2 = share(mine2, got2, send2, recv2)
    for c in late:
        c.wait()
    planes[...] = jnp.dot(plane[...], level[...], preferred_element_type=F32).astype(BF16)

    @pl.when(me == 0)
    def _():
        conv2a[0] = sum_of(conv2[0], conv2[1], conv2[2])
        conv2a[1] = sum_of(conv2[0], conv2[1])
        for i in range(9):
            down2a[i] = sum_of(down2[0, i], down2[1, i], down2[2, i])

    norms(sums2, copies2, got2, gain2_ref, shift2_ref, per_frame / 4, p2)

    row = lax.broadcasted_iota(jnp.int32, (128, 128), 0)

    def back_y(v, row):
        return jnp.where(row % 16 < 4, 0.0, pltpu.roll(v, 4, axis=0))

    def back_x(v, row):
        return jnp.where(row % 4 < 1, 0.0, pltpu.roll(v, 1, axis=0))

    def on_y(v, row):
        return jnp.where(row % 16 >= 12, 0.0, pltpu.roll(v, 124, axis=0))

    def on_x(v, row):
        return jnp.where(row % 4 >= 3, 0.0, pltpu.roll(v, 127, axis=0))

    for f in range(2):
        scale = p2[f, 0].reshape(OWN, 1, 128)
        bias = p2[f, 1].reshape(OWN, 1, 128)
        for yp in range(2):
            for xp in range(2):
                q = yp * 2 + xp
                v = planes[q * 128 : q * 128 + 128, f * 128 : f * 128 + 128].astype(F32)
                h = silu_of_half(v.reshape(OWN, 16, 128) * scale + bias).reshape(128, 128)
                hy = (back_y if yp else on_y)(h, row)
                move_x = back_x if xp else on_x
                for s, u in enumerate((h, move_x(h, row), hy, move_x(hy, row))):
                    blocks[f, q * 4 + s] = u.astype(BF16)

    taps = (((1, 1), (0, 0), (1, 0)), ((0, 0), (1, 0), (0, 1)))

    def gathered(f):
        rows = []
        for yp in range(2):
            for xp in range(2):
                cells = []
                for b in range(3):
                    for c in range(3):
                        (py, sy), (px, sx) = taps[yp][b], taps[xp][c]
                        cells.append(blocks[f, (py * 2 + px) * 4 + sy * 2 + sx])
                rows.append(jnp.concatenate(cells, axis=1))
        return jnp.concatenate(rows, axis=0)

    row2 = lax.broadcasted_iota(jnp.int32, (128, 256), 0)

    def spread(which, acc):
        u = [acc[q * 128 : q * 128 + 128] for q in range(4)]
        u1x, u3x, u2y, u3y = back_x(u[1], row2), back_x(u[3], row2), back_y(u[2], row2), back_y(u[3], row2)
        u3yx = back_x(u3y, row2)
        for i, v in enumerate((u3yx, u2y, u3y, u1x, u[0], u[1], u3x, u[2], u[3])):
            ublocks[which, i] = v.astype(BF16)

    def dot(a, b):
        return jnp.dot(a, b, preferred_element_type=F32)

    spread(3, dot(gathered(1), conv2[0]))
    spread(2, dot(gathered(0), conv2[0]) + dot(gathered(1), conv2[1]))

    def down_sum(terms):
        acc = jnp.zeros((128, 256), F32)
        for which, w in terms:
            for i in range(9):
                acc = acc + dot(ublocks[which, i], w[i])
        return acc

    next2[1] = down_sum(((2, down2.at[0]), (3, down2.at[1]))).astype(SENT2)
    skip_copy = remote(next2.at[1], part2.at[1], sems.at[12], sems.at[13], {"tm": lax.rem(me + 2, n)})
    skip_copy.start()
    spread(1, dot(gathered(0), conv2a[1]) + dot(gathered(1), conv2[2]) + dot(planes[:, second], short[...]))
    spread(0, dot(gathered(0), conv2a[0]) + dot(planes[:, first], short[...]))
    next2[0] = down_sum(((0, down2.at[0]), (1, down2.at[1]), (2, down2.at[2]))).astype(SENT2)
    next_copy = remote(next2.at[0], part2.at[0], sems.at[14], sems.at[15], {"tm": lax.rem(me + 1, n)})
    next_copy.start()
    own = down_sum(((0, down2a),))
    info_copy.wait()
    low_lane = lane < half * 16
    its_heavy = rinfo[2:3, :] == cap
    my_ids = jnp.where(low_lane | heavy, info[0:1, :], rinfo[1:2, :])
    its_ids = jnp.where(low_lane | its_heavy, rinfo[0:1, :], info[1:2, :])
    wanted = lax.axis_index("tile") * OWN + row // 16
    cell = row % 16 == lax.broadcasted_iota(jnp.int32, (128, 128), 1) % 16
    mine = jnp.where((wanted == my_ids) & cell, 1.0, 0.0).astype(BF16)
    its = jnp.where((wanted == its_ids) & cell, 1.0, 0.0).astype(BF16)
    skip_copy.wait()
    own = own + jnp.where(me > 1, part2[1].astype(F32), 0.0)
    next_copy.wait()
    enc[...] = (own + jnp.where(me > 0, part2[0].astype(F32), 0.0)).astype(BF16)
    enc_copy = swap(enc, renc, 1)
    enc_copy.start()
    kept = dot(mine, enc[...])
    enc_copy.wait()
    out_ref[...] = (kept + dot(its, renc[...])).astype(BF16)


def encode(acts, ids, counts, params, n):
    (
        first_gain,
        first_shift,
        first_conv,
        first_down,
        second_gain,
        second_shift,
        second_conv,
        second_short,
        second_down,
    ) = params
    cells = acts.shape[2:]
    rows = OWN * 64
    vm = pltpu.VMEM
    line = lambda v: v.reshape(1, 128)
    return pl.pallas_call(
        functools.partial(main_kernel, n, float(cells[0] * cells[1] * (cells[2] // GROUPS))),
        out_shape=jax.ShapeDtypeStruct((OWN * 16, 256), BF16),
        in_specs=[ANY, SMEM, SMEM, VMEM, VMEM, ANY, ANY, VMEM, VMEM, ANY, ANY, ANY, ANY],
        out_specs=VMEM,
        scratch_shapes=[
            vm((4, OWN) + cells, BF16),
            vm((4, MOVED) + cells, BF16),
            vm((8, 128), jnp.int32),
            vm((8, 128), jnp.int32),
            vm((4, 2 * OWN, 128), F32),
            vm((3, 1152, 256), BF16),
            vm((2, 1152, 256), BF16),
            vm((128, 256), BF16),
            vm((3, 9, 256, 256), BF16),
            vm((9, 256, 256), BF16),
            vm((rows, rows), BF16),
            vm((2 * OWN, 128), F32),
            vm((n, 2 * OWN, 128), F32),
            vm((2 * OWN, 128), F32),
            vm((n, 2 * OWN, 128), F32),
            vm((4, 2, OWN, 128), F32),
            vm((2, 2, OWN, 128), F32),
            vm((3, 2, 560, 768), BF16),
            vm((2, 2, 560, 768), BF16),
            vm((3, 768, 256), BF16),
            vm((3, 768, 256), BF16),
            vm((3, 768, 256), BF16),
            vm((3, 768, 256), BF16),
            vm((3, 768, 256), BF16),
            vm((2, 3, 2, 512, 128), F32),
            vm((3, 3, rows, 768), BF16),
            vm((3, rows, 256), F32),
            vm((2, 2, 256, 128), SENT1),
            vm((2, 2, 256, 128), SENT1),
            vm((rows, 256), BF16),
            vm((rows, 256), BF16),
            vm((2, 16, 128, 128), BF16),
            vm((4, 9, 128, 256), BF16),
            vm((2, OWN * 16, 256), SENT2),
            vm((2, OWN * 16, 256), SENT2),
            vm((OWN * 16, 256), BF16),
            vm((OWN * 16, 256), BF16),
            pltpu.SemaphoreType.DMA((n,)),
            pltpu.SemaphoreType.DMA((n,)),
            pltpu.SemaphoreType.DMA((n,)),
            pltpu.SemaphoreType.DMA((n,)),
            pltpu.SemaphoreType.DMA((2,)),
            pltpu.SemaphoreType.DMA((2,)),
            pltpu.SemaphoreType.DMA((16,)),
            pltpu.SemaphoreType.DMA((24,)),
        ],
        name="encode",
        compiler_params=pltpu.CompilerParams(collective_id=0, has_side_effects=True, vmem_limit_bytes=LIMIT),
    )(
        acts,
        ids,
        counts,
        line(first_gain),
        line(first_shift),
        first_conv.reshape(3, 3, 384, 128),
        first_down.reshape(3, 3, 384, 128),
        line(second_gain),
        line(second_shift),
        second_conv.reshape(3, 1152, 256),
        second_short,
        second_down.reshape(3, 9, 256, 256),
        jnp.asarray(plane_matrix(), BF16),
    )


def body(activations, tile_ids, tile_counts, *params):
    n = lax.axis_size("tm")
    latents = encode(activations, tile_ids, tile_counts, params, n)
    return latents.reshape(1, OWN, 4, 4, 256)


def solution(mesh):
    placed = (
        P(("groups", "tm"), "tile", None, None, None),
        P(("groups", "tile")),
        P(("groups", "tile")),
    ) + (P(),) * 9
    return jax.shard_map(
        body,
        mesh=mesh,
        in_specs=placed,
        out_specs=P(("groups", "tm"), "tile", None, None, None),
        check_vma=False,
    )
```

```python
import functools

import jax
import jax.numpy as jnp
import numpy as np
from jax import lax
from jax.experimental import pallas as pl
from jax.experimental.pallas import tpu as pltpu
from jax.sharding import PartitionSpec as P

GROUPS = 32
OWN = 8
MOVED = 4
EPS = 1e-06
F32 = jnp.float32
BF16 = jnp.bfloat16
SENT1 = jnp.bfloat16
SENT2 = jnp.bfloat16
MESH = pl.DeviceIdType.MESH
VMEM = pl.BlockSpec(memory_space=pltpu.VMEM)
SMEM = pl.BlockSpec(memory_space=pltpu.SMEM)
ANY = pl.BlockSpec(memory_space=pl.ANY)
LIMIT = 56 << 20


def silu_of_half(w):
    return w + w * jnp.tanh(w)


def dot(a, b):
    return jnp.dot(a, b, preferred_element_type=F32)


def shifted(v, side):
    rows = v.shape[0]
    col = lax.broadcasted_iota(jnp.int32, v.shape, 0) % side
    left = jnp.where(col == 0, 0.0, pltpu.roll(v, 1, axis=0))
    right = jnp.where(col == side - 1, 0.0, pltpu.roll(v, rows - 1, axis=0))
    return left, right


def plane_matrix():
    m = np.zeros((2, 2, OWN, 4, 4, OWN, 8, 8), np.float32)
    for yp in range(2):
        for xp in range(2):
            for t in range(OWN):
                for y in range(4):
                    for x in range(4):
                        m[yp, xp, t, y, x, t, 2 * y + yp, 2 * x + xp] = 1.0
    return m.reshape(OWN * 64, OWN * 64)


def main_kernel(
    n,
    per_frame,
    act_ref,
    ids_ref,
    count_ref,
    gain1_ref,
    shift1_ref,
    conv1_hbm,
    down1_hbm,
    gain2_ref,
    shift2_ref,
    conv2_hbm,
    short_hbm,
    down2_hbm,
    plane_hbm,
    out_ref,
    x,
    moved,
    info,
    rinfo,
    s_ref,
    conv2,
    conv2a,
    short,
    down2,
    down2a,
    plane,
    mine1,
    got1,
    mine2,
    got2,
    p1,
    p2,
    bufe,
    bufo,
    ws,
    wn,
    wa,
    wd,
    wda,
    sf,
    lhs,
    outd,
    next1,
    part1,
    level,
    planes,
    blocks,
    ublocks,
    next2,
    part2,
    enc,
    renc,
    send1,
    recv1,
    send2,
    recv2,
    psend,
    precv,
    sems,
    local,
):
    me = lax.axis_index("tm")
    partner = 1 - lax.axis_index("tile")
    cap = act_ref.shape[1]
    used = [0]

    def copy_in(src, dst):
        c = pltpu.make_async_copy(src, dst, local.at[used[0]])
        used[0] += 1
        return c

    half = OWN - MOVED
    fetch = [
        copy_in(act_ref.at[:, 0:half], x.at[:, 0:half]),
        copy_in(act_ref.at[:, half:OWN], x.at[:, half:OWN]),
    ]
    for c in fetch:
        c.start()
    barrier = pltpu.get_barrier_semaphore()
    pl.semaphore_signal(barrier, inc=1, device_id={"tile": partner}, device_id_type=MESH)

    def greet(k, _):
        pl.semaphore_signal(barrier, inc=1, device_id={"tm": me - k}, device_id_type=MESH)
        return 0

    lax.fori_loop(1, me + 1, greet, 0)

    lane = lax.broadcasted_iota(jnp.int32, (1, 128), 1)
    count = count_ref[0]
    heavy = jnp.full((1, 128), count, jnp.int32) == cap

    def remote(src, dst, send_sem, recv_sem, target):
        return pltpu.make_async_remote_copy(
            src_ref=src, dst_ref=dst, send_sem=send_sem, recv_sem=recv_sem, device_id=target, device_id_type=MESH
        )

    def swap(src, dst, i):
        return remote(src, dst, sems.at[2 * i], sems.at[2 * i + 1], {"tile": partner})

    quarter = lax.broadcasted_iota(jnp.int32, (4, 128), 1) % 4

    def grouped_sums(sums):
        ri = lax.broadcasted_iota(jnp.int32, (128, 128), 0) // (128 // GROUPS)
        ci = lax.broadcasted_iota(jnp.int32, (128, 128), 1) // (128 // GROUPS)
        same = jnp.where(ri == ci, 1.0, 0.0).astype(F32)
        rows = jnp.dot(
            jnp.concatenate(sums, axis=0), same, precision=lax.Precision.HIGHEST, preferred_element_type=F32
        )
        return [rows[f * 2 * OWN : (f + 1) * 2 * OWN] for f in range(len(sums))]

    def packed(rows):
        total = rows[0]
        for r in rows[1:]:
            total = total + r
        v = total[0:4]
        for q in range(1, 4):
            v = jnp.where(quarter == q, total[4 * q : 4 * q + 4], v)
        return v

    def unpacked(v):
        parts = [jnp.where(quarter == 0, v, 0.0)]
        for q in range(1, 4):
            parts.append(pltpu.roll(jnp.where(quarter == q, v, 0.0), 128 - q, axis=1))
        w = jnp.concatenate(parts, axis=0)
        w = w + pltpu.roll(w, 1, axis=1)
        return w + pltpu.roll(w, 2, axis=1)

    def sum_copy(mine, got, sent, here, k):
        return remote(mine, got.at[k], sent.at[k], here.at[k], {"tm": me + k})

    def share(mine, got, sent, here):
        def start(i, _):
            sum_copy(mine, got, sent, here, n - me - i).start()
            return 0

        lax.fori_loop(1, n - me, start, 0)

    def shared(mine, got, sent, here):
        def wait(k, _):
            sum_copy(mine, got, sent, here, k).wait_send()
            return 0

        lax.fori_loop(1, n - me, wait, 0)

    def norms(rows, mine, got, sent, here, gain, shift, size, out):
        def take(k, run):
            sum_copy(mine, got, sent, here, k).wait_recv()
            return run + got[k]

        run = unpacked(lax.fori_loop(1, me + 1, take, jnp.zeros((4, 128), F32)))
        start = (me * len(rows)).astype(F32)
        for i, r in enumerate(rows):
            run = run + r
            inv_count = jnp.full((1, 128), 1.0, F32) / (jnp.zeros((1, 128), F32) + (start + float(i + 1)) * size)
            m = run[0:OWN] * inv_count
            var = run[OWN : 2 * OWN] * inv_count - m * m
            scale = lax.rsqrt(var + EPS) * gain[...]
            out[i, 0] = 0.5 * scale
            out[i, 1] = 0.5 * (shift[...] - m * scale)

    pl.semaphore_wait(barrier, n - me)
    move_copies = [swap(act_ref.at[:, OWN + i], moved.at[:, i], 2 + i) for i in range(MOVED)]
    for c in move_copies:
        c.start()
    zero = jnp.zeros((384, 128), BF16)
    for b in range(3):
        ws[b, 384:768, 0:128] = zero
        wa[b, 384:768, 0:128] = zero
        wn[b, 0:384, 128:256] = zero
        wd[b, 384:768, 0:128] = zero
        wda[b, 384:768, 0:128] = zero
    edge = jnp.zeros((16, 768), BF16)
    for tiles in (bufe, bufo):
        for i in range(2):
            for p in range(2):
                for r in (0, 272, 544):
                    tiles[i, p, r : r + 16] = edge


    @pl.when(me == 0)
    def _():
        part1[...] = jnp.zeros_like(part1)
        part2[...] = jnp.zeros_like(part2)

    @pl.when(me == 1)
    def _():
        part2[1] = jnp.zeros_like(part2[1])

    top, low = slice(0, 384), slice(384, 768)
    first, second = slice(0, 128), slice(128, 256)
    early = [
        copy_in(h.at[a], w.at[:, r, c])
        for h, a, w, r, c in (
            (conv1_hbm, 0, wn, top, first),
            (conv1_hbm, 1, wn, low, first),
            (conv1_hbm, 0, wn, low, second),
            (conv1_hbm, 2, ws, top, first),
            (conv1_hbm, 1, ws, top, second),
            (conv1_hbm, 2, ws, low, second),
            (conv1_hbm, 2, wa, top, first),
            (conv1_hbm, 1, wa, top, second),
            (conv1_hbm, 2, wa, low, second),
            (down1_hbm, 2, wd, top, first),
            (down1_hbm, 0, wd, top, second),
            (down1_hbm, 1, wd, low, second),
            (down1_hbm, 2, wda, top, first),
            (down1_hbm, 0, wda, top, second),
            (down1_hbm, 1, wda, low, second),
        )
    ]
    late = [
        copy_in(a, b)
        for a, b in (
            (plane_hbm, plane),
            (conv2_hbm, conv2),
            (conv2_hbm.at[2], conv2a.at[0]),
            (conv2_hbm.at[1], conv2a.at[1]),
            (short_hbm, short),
            (down2_hbm, down2),
            (down2_hbm.at[2], down2a),
        )
    ]

    def add_up(f, j, v):
        s_ref[f, pl.ds(j, 1), :] = jnp.sum(v, axis=0, keepdims=True)
        s_ref[f, pl.ds(OWN + j, 1), :] = jnp.sum(v * v, axis=0, keepdims=True)

    fetch[0].wait()

    def count_own(j, _):
        for f in range(4):
            add_up(f, j, x[f, j].astype(F32).reshape(256, 128))
        return 0

    lax.fori_loop(0, half, count_own, 0)
    fetch[1].wait()
    for c in early:
        c.start()
    for i in range(MOVED):
        move_copies[i].wait()

    def count_moved(i, _):
        j = half + i
        for f in range(4):
            a = x[f, j].astype(F32).reshape(256, 128)
            v = jnp.where(heavy, a, moved[f, i].astype(F32).reshape(256, 128))
            x[f, j] = v.astype(BF16).reshape(x.shape[2:])
            add_up(f, j, v)
        return 0

    lax.fori_loop(0, MOVED, count_moved, 0)
    rows1 = grouped_sums([s_ref[f] for f in range(4)])
    mine1[...] = packed(rows1)
    share(mine1, got1, send1, recv1)
    def row_ids(slots):
        v = jnp.full((1, 128), -1, jnp.int32)
        for j, slot in enumerate(slots):
            v = jnp.where(lane // 16 == j, jnp.where(slot < count, ids_ref[slot], -1), v)
        return v

    info[0:1] = row_ids(range(OWN))
    info[1:2] = row_ids(list(range(half)) + list(range(OWN, OWN + MOVED)))
    info[2:8] = jnp.full((6, 128), count, jnp.int32)
    info_copy = swap(info, rinfo, 0)
    info_copy.start()
    for c in late:
        c.start()
    for c in early:
        c.wait()

    def sum_of(*refs):
        total = refs[0].astype(F32)
        for r in refs[1:]:
            total = total + r.astype(F32)
        return total.astype(BF16)

    @pl.when(me == 0)
    def _():
        for b in range(3):
            k0, k1, k2 = wn[b, top, first], ws[b, top, second], ws[b, top, first]
            wa[b, top, first] = sum_of(k0, k1, k2)
            wa[b, top, second] = sum_of(k0, k1)
            wda[b, top, first] = sum_of(wd[b, top, first], wd[b, top, second], wd[b, low, second])

    norms(rows1, mine1, got1, send1, recv1, gain1_ref, shift1_ref, per_frame, p1)

    def prep(i, tiles):
        for t in range(2):
            j = 2 * i + t
            rows = slice(16 + t * 272, 272 + t * 272)
            for q in range(4):
                v = x[q, j].astype(F32).reshape(256, 128)
                h = silu_of_half(v * p1[q, 0, pl.ds(j, 1), :] + p1[q, 1, pl.ds(j, 1), :])
                left, right = shifted(h, 16)
                k = (q % 2) * 384
                tiles[q // 2, rows, k : k + 128] = left.astype(BF16)
                tiles[q // 2, rows, k + 128 : k + 256] = h.astype(BF16)
                tiles[q // 2, rows, k + 256 : k + 384] = right.astype(BF16)

    def conv(tiles, terms):
        acc = jnp.zeros((512, 256), F32)
        for p, w in terms:
            for b in range(3):
                r = b * 16
                pair = jnp.concatenate([tiles[p, r : r + 256, :], tiles[p, r + 272 : r + 528, :]], axis=0)
                acc = acc + jnp.dot(pair, w[b], preferred_element_type=F32)
        return acc

    def build(i, z, which, acc, frame):
        col = lax.broadcasted_iota(jnp.int32, (256, 128), 0) % 8
        rows = pl.ds(pl.multiple_of(i * 128, 128), 128)
        for e in range(2):
            for t in range(2):
                v = acc[t * 256 : t * 256 + 256, e * 128 : e * 128 + 128]
                if frame is not None:
                    v = v + x[frame + e, 2 * i + t].astype(F32).reshape(256, 128)
                sf[z, which, e, t * 256 : t * 256 + 256] = v
        for e in range(2):
            even = sf[z, which, e, pl.ds(0, 256, stride=2), :]
            odd = sf[z, which, e, pl.ds(1, 256, stride=2), :]
            prev = jnp.where(col == 0, 0.0, pltpu.roll(odd, 1, axis=0))
            for c, v in enumerate((prev, even, odd)):
                v = v.reshape(2, 8, 2, 8, 128)
                up_rows, low_rows = v[:, :, 0], v[:, :, 1]
                above = jnp.concatenate([jnp.zeros((2, 1, 8, 128), F32), low_rows[:, :7]], axis=1)
                k = e * 384 + c * 128
                for b, u in enumerate((above, up_rows, low_rows)):
                    lhs[which, b, rows, k : k + 128] = u.reshape(128, 128).astype(BF16)

    pairs = OWN // 2

    def part_copy(i):
        return remote(next1.at[i], part1.at[i], psend.at[i], precv.at[i], {"tm": me + 1})

    def step(i, _):
        def onward(pair, z, tiles):
            build(pair, z, 2, conv(tiles, ((1, wn),)), None)
            build(pair, z, 1, conv(tiles, ((1, ws), (0, wn))), 2)

        prep(2 * i + 1, bufo.at[i])
        onward(2 * i, 0, bufe.at[i])
        prep(jnp.minimum(2 * i + 2, pairs - 1), bufe.at[i + 1])
        onward(2 * i + 1, 1, bufo.at[i])
        rows = pl.ds(pl.multiple_of(i * 256, 256), 256)

        @pl.when(me < n)
        def _():
            both = [jnp.concatenate([lhs[1, b, rows, :], lhs[2, b, rows, :]], axis=0) for b in range(3)]
            out = dot(both[0], wd[0]) + dot(both[1], wd[1]) + dot(both[2], wd[2])
            outd[1, rows, :] = out[0:256]
            outd[2, rows, :] = out[256:512]

        next1[i, 0] = (outd[1, rows, second] + outd[2, rows, first]).astype(SENT1)
        next1[i, 1] = outd[2, rows, second].astype(SENT1)

        @pl.when(me < n - 1)
        def _():
            part_copy(i).start()

        return 0

    prep(0, bufe.at[0])
    lax.fori_loop(0, 2, step, 0)

    def own_step(i, _):
        build(2 * i, 0, 0, conv(bufe.at[i], ((0, wa),)), 0)
        build(2 * i + 1, 1, 0, conv(bufo.at[i], ((0, wa),)), 0)
        return 0

    lax.fori_loop(0, 2, own_step, 0)
    outd[0] = dot(lhs[0, 0], wda[0]) + dot(lhs[0, 1], wda[1]) + dot(lhs[0, 2], wda[2])
    for i in range(2):

        @pl.when(me > 0)
        def _():
            part_copy(i).wait_recv()

        rows = slice(i * 256, i * 256 + 256)
        for f in range(2):
            v = outd[0, rows, f * 128 : f * 128 + 128]
            if f == 1:
                v = v + outd[1, rows, first]
            v = v + part1[i, f].astype(F32)
            level[rows, f * 128 : f * 128 + 128] = v.astype(BF16)
    sums2 = []
    for f in range(2):
        v = level[:, f * 128 : f * 128 + 128].astype(F32).reshape(OWN, 64, 128)
        sums2.append(jnp.concatenate([jnp.sum(v, axis=1), jnp.sum(v * v, axis=1)], axis=0))
    rows2 = grouped_sums(sums2)
    mine2[...] = packed(rows2)
    share(mine2, got2, send2, recv2)
    for c in late:
        c.wait()
    planes[...] = jnp.dot(plane[...], level[...], preferred_element_type=F32).astype(BF16)

    @pl.when(me == 0)
    def _():
        conv2a[0] = sum_of(conv2[0], conv2[1], conv2[2])
        conv2a[1] = sum_of(conv2[0], conv2[1])
        for i in range(9):
            down2a[i] = sum_of(down2[0, i], down2[1, i], down2[2, i])

    norms(rows2, mine2, got2, send2, recv2, gain2_ref, shift2_ref, per_frame / 4, p2)

    row = lax.broadcasted_iota(jnp.int32, (128, 128), 0)

    def back_y(v, row):
        return jnp.where(row % 16 < 4, 0.0, pltpu.roll(v, 4, axis=0))

    def back_x(v, row):
        return jnp.where(row % 4 < 1, 0.0, pltpu.roll(v, 1, axis=0))

    def on_y(v, row):
        return jnp.where(row % 16 >= 12, 0.0, pltpu.roll(v, 124, axis=0))

    def on_x(v, row):
        return jnp.where(row % 4 >= 3, 0.0, pltpu.roll(v, 127, axis=0))

    for f in range(2):
        scale = p2[f, 0].reshape(OWN, 1, 128)
        bias = p2[f, 1].reshape(OWN, 1, 128)
        for yp in range(2):
            for xp in range(2):
                q = yp * 2 + xp
                v = planes[q * 128 : q * 128 + 128, f * 128 : f * 128 + 128].astype(F32)
                h = silu_of_half(v.reshape(OWN, 16, 128) * scale + bias).reshape(128, 128)
                hy = (back_y if yp else on_y)(h, row)
                move_x = back_x if xp else on_x
                for s, u in enumerate((h, move_x(h, row), hy, move_x(hy, row))):
                    blocks[f, q * 4 + s] = u.astype(BF16)

    taps = (((1, 1), (0, 0), (1, 0)), ((0, 0), (1, 0), (0, 1)))

    def gathered(f):
        rows = []
        for yp in range(2):
            for xp in range(2):
                cells = []
                for b in range(3):
                    for c in range(3):
                        (py, sy), (px, sx) = taps[yp][b], taps[xp][c]
                        cells.append(blocks[f, (py * 2 + px) * 4 + sy * 2 + sx])
                rows.append(jnp.concatenate(cells, axis=1))
        return jnp.concatenate(rows, axis=0)

    row2 = lax.broadcasted_iota(jnp.int32, (128, 256), 0)

    def spread(which, acc):
        u = [acc[q * 128 : q * 128 + 128] for q in range(4)]
        u1x, u3x, u2y, u3y = back_x(u[1], row2), back_x(u[3], row2), back_y(u[2], row2), back_y(u[3], row2)
        u3yx = back_x(u3y, row2)
        for i, v in enumerate((u3yx, u2y, u3y, u1x, u[0], u[1], u3x, u[2], u[3])):
            ublocks[which, i] = v.astype(BF16)

    spread(3, dot(gathered(1), conv2[0]))
    spread(2, dot(gathered(0), conv2[0]) + dot(gathered(1), conv2[1]))

    def down_sum(terms):
        acc = jnp.zeros((128, 256), F32)
        for which, w in terms:
            for i in range(9):
                acc = acc + dot(ublocks[which, i], w[i])
        return acc

    skip_copy = remote(next2.at[1], part2.at[1], sems.at[12], sems.at[13], {"tm": me + 2})
    next_copy = remote(next2.at[0], part2.at[0], sems.at[14], sems.at[15], {"tm": me + 1})

    @pl.when(me < n - 2)
    def _():
        next2[1] = down_sum(((2, down2.at[0]), (3, down2.at[1]))).astype(SENT2)
        skip_copy.start()

    spread(1, dot(gathered(0), conv2a[1]) + dot(gathered(1), conv2[2]) + dot(planes[:, second], short[...]))
    spread(0, dot(gathered(0), conv2a[0]) + dot(planes[:, first], short[...]))

    @pl.when(me < n - 1)
    def _():
        next2[0] = down_sum(((0, down2.at[0]), (1, down2.at[1]), (2, down2.at[2]))).astype(SENT2)
        next_copy.start()

    own = down_sum(((0, down2a),))
    info_copy.wait()
    low_lane = lane < half * 16
    its_heavy = rinfo[2:3, :] == cap
    my_ids = jnp.where(low_lane | heavy, info[0:1, :], rinfo[1:2, :])
    its_ids = jnp.where(low_lane | its_heavy, rinfo[0:1, :], info[1:2, :])
    wanted = lax.axis_index("tile") * OWN + row // 16
    cell = row % 16 == lax.broadcasted_iota(jnp.int32, (128, 128), 1) % 16
    mine = jnp.where((wanted == my_ids) & cell, 1.0, 0.0).astype(BF16)
    its = jnp.where((wanted == its_ids) & cell, 1.0, 0.0).astype(BF16)

    @pl.when(me > 1)
    def _():
        skip_copy.wait_recv()

    @pl.when(me > 0)
    def _():
        next_copy.wait_recv()

    enc[...] = (own + part2[1].astype(F32) + part2[0].astype(F32)).astype(BF16)
    enc_copy = swap(enc, renc, 1)
    enc_copy.start()
    kept = dot(mine, enc[...])
    shared(mine1, got1, send1, recv1)
    shared(mine2, got2, send2, recv2)

    @pl.when(me < n - 1)
    def _():
        for i in range(2):
            part_copy(i).wait_send()
        next_copy.wait_send()

    @pl.when(me < n - 2)
    def _():
        skip_copy.wait_send()

    enc_copy.wait()
    out_ref[...] = (kept + dot(its, renc[...])).astype(BF16).reshape(out_ref.shape)


def encode(acts, ids, counts, params, n):
    (
        first_gain,
        first_shift,
        first_conv,
        first_down,
        second_gain,
        second_shift,
        second_conv,
        second_short,
        second_down,
    ) = params
    cells = acts.shape[2:]
    rows = OWN * 64
    vm = pltpu.VMEM
    line = lambda v: v.reshape(1, 128)
    return pl.pallas_call(
        functools.partial(main_kernel, n, float(cells[0] * cells[1] * (cells[2] // GROUPS))),
        out_shape=jax.ShapeDtypeStruct((OWN * 4, 4, 256), BF16),
        in_specs=[ANY, SMEM, SMEM, VMEM, VMEM, ANY, ANY, VMEM, VMEM, ANY, ANY, ANY, ANY],
        out_specs=VMEM,
        scratch_shapes=[
            vm((4, OWN) + cells, BF16),
            vm((4, MOVED) + cells, BF16),
            vm((8, 128), jnp.int32),
            vm((8, 128), jnp.int32),
            vm((4, 2 * OWN, 128), F32),
            vm((3, 1152, 256), BF16),
            vm((2, 1152, 256), BF16),
            vm((128, 256), BF16),
            vm((3, 9, 256, 256), BF16),
            vm((9, 256, 256), BF16),
            vm((rows, rows), BF16),
            vm((4, 128), F32),
            vm((n, 4, 128), F32),
            vm((4, 128), F32),
            vm((n, 4, 128), F32),
            vm((4, 2, OWN, 128), F32),
            vm((2, 2, OWN, 128), F32),
            vm((3, 2, 560, 768), BF16),
            vm((2, 2, 560, 768), BF16),
            vm((3, 768, 256), BF16),
            vm((3, 768, 256), BF16),
            vm((3, 768, 256), BF16),
            vm((3, 768, 256), BF16),
            vm((3, 768, 256), BF16),
            vm((2, 3, 2, 512, 128), F32),
            vm((3, 3, rows, 768), BF16),
            vm((3, rows, 256), F32),
            vm((2, 2, 256, 128), SENT1),
            vm((2, 2, 256, 128), SENT1),
            vm((rows, 256), BF16),
            vm((rows, 256), BF16),
            vm((2, 16, 128, 128), BF16),
            vm((4, 9, 128, 256), BF16),
            vm((2, OWN * 16, 256), SENT2),
            vm((2, OWN * 16, 256), SENT2),
            vm((OWN * 16, 256), BF16),
            vm((OWN * 16, 256), BF16),
            pltpu.SemaphoreType.DMA((n,)),
            pltpu.SemaphoreType.DMA((n,)),
            pltpu.SemaphoreType.DMA((n,)),
            pltpu.SemaphoreType.DMA((n,)),
            pltpu.SemaphoreType.DMA((2,)),
            pltpu.SemaphoreType.DMA((2,)),
            pltpu.SemaphoreType.DMA((16,)),
            pltpu.SemaphoreType.DMA((24,)),
        ],
        name="encode",
        compiler_params=pltpu.CompilerParams(collective_id=0, has_side_effects=True, vmem_limit_bytes=LIMIT),
    )(
        acts,
        ids,
        counts,
        line(first_gain),
        line(first_shift),
        first_conv.reshape(3, 3, 384, 128),
        first_down.reshape(3, 3, 384, 128),
        line(second_gain),
        line(second_shift),
        second_conv.reshape(3, 1152, 256),
        second_short,
        second_down.reshape(3, 9, 256, 256),
        jnp.asarray(plane_matrix(), BF16),
    )


def body(activations, tile_ids, tile_counts, *params):
    n = lax.axis_size("tm")
    latents = encode(activations, tile_ids, tile_counts, params, n)
    return latents.reshape(1, OWN, 4, 4, 256)


def solution(mesh):
    placed = (
        P(("groups", "tm"), "tile", None, None, None),
        P(("groups", "tile")),
        P(("groups", "tile")),
    ) + (P(),) * 9
    return jax.shard_map(
        body,
        mesh=mesh,
        in_specs=placed,
        out_specs=P(("groups", "tm"), "tile", None, None, None),
        check_vma=False,
    )
```

```python
import functools

import jax
import jax.numpy as jnp
import numpy as np
from jax import lax
from jax.experimental import pallas as pl
from jax.experimental.pallas import tpu as pltpu
from jax.sharding import PartitionSpec as P

GROUPS = 32
OWN = 8
MOVED = 4
SLOTS = OWN + MOVED
EPS = 1e-06
F32 = jnp.float32
BF16 = jnp.bfloat16
SENT1 = jnp.bfloat16
SENT2 = jnp.bfloat16
MESH = pl.DeviceIdType.MESH
VMEM = pl.BlockSpec(memory_space=pltpu.VMEM)
SMEM = pl.BlockSpec(memory_space=pltpu.SMEM)
ANY = pl.BlockSpec(memory_space=pl.ANY)
LIMIT = 56 << 20


def silu_of_half(w):
    return w + w * jnp.tanh(w)


def dot(a, b):
    return jnp.dot(a, b, preferred_element_type=F32)


def shifted(v, side):
    rows = v.shape[0]
    col = lax.broadcasted_iota(jnp.int32, v.shape, 0) % side
    left = jnp.where(col == 0, 0.0, pltpu.roll(v, 1, axis=0))
    right = jnp.where(col == side - 1, 0.0, pltpu.roll(v, rows - 1, axis=0))
    return left, right


def plane_matrix():
    m = np.zeros((2, 2, OWN, 4, 4, OWN, 8, 8), np.float32)
    for yp in range(2):
        for xp in range(2):
            for t in range(OWN):
                for y in range(4):
                    for x in range(4):
                        m[yp, xp, t, y, x, t, 2 * y + yp, 2 * x + xp] = 1.0
    return m.reshape(OWN * 64, OWN * 64)


def main_kernel(
    n,
    per_frame,
    act_ref,
    ids_ref,
    count_ref,
    gain1_ref,
    shift1_ref,
    conv1_hbm,
    down1_hbm,
    gain2_ref,
    shift2_ref,
    conv2_hbm,
    short_hbm,
    down2_hbm,
    plane_hbm,
    out_ref,
    x,
    moved,
    gift,
    given,
    info,
    rinfo,
    s_ref,
    conv2,
    conv2a,
    short,
    down2,
    down2a,
    plane,
    mine1,
    got1,
    mine2,
    got2,
    p1,
    p2,
    bufe,
    bufo,
    ws,
    wn,
    wa,
    wd,
    wda,
    sf,
    lhs,
    outd,
    next1,
    part1,
    level,
    planes,
    blocks,
    ublocks,
    next2,
    part2,
    enc,
    renc,
    send1,
    recv1,
    send2,
    recv2,
    psend,
    precv,
    sems,
    local,
):
    me = lax.axis_index("tm")
    partner = 1 - lax.axis_index("tile")
    cap = act_ref.shape[1]
    used = [0]

    def copy_in(src, dst):
        c = pltpu.make_async_copy(src, dst, local.at[used[0]])
        used[0] += 1
        return c

    half = OWN - MOVED
    fetch = [
        copy_in(act_ref.at[:, 0:half], x.at[:, 0:half]),
        copy_in(act_ref.at[:, half:OWN], x.at[:, half:OWN]),
        copy_in(act_ref.at[:, OWN : OWN + MOVED], x.at[:, OWN : OWN + MOVED]),
    ]
    for c in fetch:
        c.start()
    barrier = pltpu.get_barrier_semaphore()
    pl.semaphore_signal(barrier, inc=1, device_id={"tile": partner}, device_id_type=MESH)

    def greet(k, _):
        pl.semaphore_signal(barrier, inc=1, device_id={"tm": me - k}, device_id_type=MESH)
        return 0

    lax.fori_loop(1, me + 1, greet, 0)

    lane = lax.broadcasted_iota(jnp.int32, (1, 128), 1)
    count = count_ref[0]
    heavy = jnp.full((1, 128), count, jnp.int32) == cap

    def remote(src, dst, send_sem, recv_sem, target):
        return pltpu.make_async_remote_copy(
            src_ref=src, dst_ref=dst, send_sem=send_sem, recv_sem=recv_sem, device_id=target, device_id_type=MESH
        )

    def swap(src, dst, i):
        return remote(src, dst, sems.at[2 * i], sems.at[2 * i + 1], {"tile": partner})

    quarter = lax.broadcasted_iota(jnp.int32, (4, 128), 1) % 4

    def grouped_sums(sums):
        ri = lax.broadcasted_iota(jnp.int32, (128, 128), 0) // (128 // GROUPS)
        ci = lax.broadcasted_iota(jnp.int32, (128, 128), 1) // (128 // GROUPS)
        same = jnp.where(ri == ci, 1.0, 0.0).astype(F32)
        rows = jnp.dot(
            jnp.concatenate(sums, axis=0), same, precision=lax.Precision.HIGHEST, preferred_element_type=F32
        )
        size = sums[0].shape[0]
        return [rows[f * size : (f + 1) * size] for f in range(len(sums))]

    def packed(rows):
        total = rows[0]
        for r in rows[1:]:
            total = total + r
        v = total[0:4]
        for q in range(1, 4):
            v = jnp.where(quarter == q, total[4 * q : 4 * q + 4], v)
        return v

    def unpacked(v):
        parts = [jnp.where(quarter == 0, v, 0.0)]
        for q in range(1, 4):
            parts.append(pltpu.roll(jnp.where(quarter == q, v, 0.0), 128 - q, axis=1))
        w = jnp.concatenate(parts, axis=0)
        w = w + pltpu.roll(w, 1, axis=1)
        return w + pltpu.roll(w, 2, axis=1)

    top, low = slice(0, 384), slice(384, 768)
    first, second = slice(0, 128), slice(128, 256)

    def sum_copy(mine, got, sent, here, k):
        return remote(mine, got.at[k], sent.at[k], here.at[k], {"tm": me + k})

    def share(mine, got, sent, here):
        def start(i, _):
            sum_copy(mine, got, sent, here, n - me - i).start()
            return 0

        lax.fori_loop(1, n - me, start, 0)

    def shared(mine, got, sent, here):
        def wait(k, _):
            sum_copy(mine, got, sent, here, k).wait_send()
            return 0

        lax.fori_loop(1, n - me, wait, 0)

    def norms(rows, mine, got, sent, here, gain, shift, size, out):
        def take(k, run):
            sum_copy(mine, got, sent, here, k).wait_recv()
            return run + got[k]

        run = unpacked(lax.fori_loop(1, me + 1, take, jnp.zeros((4, 128), F32)))
        start = (me * len(rows)).astype(F32)
        for i, r in enumerate(rows):
            run = run + r
            inv_count = jnp.full((1, 128), 1.0, F32) / (jnp.zeros((1, 128), F32) + (start + float(i + 1)) * size)
            m = run[0:OWN] * inv_count
            var = run[OWN : 2 * OWN] * inv_count - m * m
            scale = lax.rsqrt(var + EPS) * gain[...]
            out[i, 0] = 0.5 * scale
            out[i, 1] = 0.5 * (shift[...] - m * scale)

    zero = jnp.zeros((384, 128), BF16)
    for b in range(3):
        ws[b, 384:768, 0:128] = zero
        wa[b, 384:768, 0:128] = zero
        wn[b, 0:384, 128:256] = zero
        wd[b, 384:768, 0:128] = zero
        wda[b, 384:768, 0:128] = zero
    edge = jnp.zeros((16, 768), BF16)
    for tiles in (bufe, bufo):
        for i in range(2):
            for p in range(2):
                for r in (0, 272, 544):
                    tiles[i, p, r : r + 16] = edge


    @pl.when(me == 0)
    def _():
        part1[...] = jnp.zeros_like(part1)
        part2[...] = jnp.zeros_like(part2)

    @pl.when(me == 1)
    def _():
        part2[1] = jnp.zeros_like(part2[1])

    early = [
        copy_in(h.at[a], w.at[:, r, c])
        for h, a, w, r, c in (
            (conv1_hbm, 0, wn, top, first),
            (conv1_hbm, 1, wn, low, first),
            (conv1_hbm, 0, wn, low, second),
            (conv1_hbm, 2, ws, top, first),
            (conv1_hbm, 1, ws, top, second),
            (conv1_hbm, 2, ws, low, second),
            (conv1_hbm, 2, wa, top, first),
            (conv1_hbm, 1, wa, top, second),
            (conv1_hbm, 2, wa, low, second),
            (down1_hbm, 2, wd, top, first),
            (down1_hbm, 0, wd, top, second),
            (down1_hbm, 1, wd, low, second),
            (down1_hbm, 2, wda, top, first),
            (down1_hbm, 0, wda, top, second),
            (down1_hbm, 1, wda, low, second),
        )
    ]
    late = [
        copy_in(a, b)
        for a, b in (
            (plane_hbm, plane),
            (conv2_hbm, conv2),
            (conv2_hbm.at[2], conv2a.at[0]),
            (conv2_hbm.at[1], conv2a.at[1]),
            (short_hbm, short),
            (down2_hbm, down2),
            (down2_hbm.at[2], down2a),
        )
    ]

    def add_up(f, j, v):
        s_ref[f, pl.ds(j, 1), :] = jnp.sum(v, axis=0, keepdims=True)
        s_ref[f, pl.ds(SLOTS + j, 1), :] = jnp.sum(v * v, axis=0, keepdims=True)

    def count_slot(j, _):
        for f in range(4):
            add_up(f, j, x[f, j].astype(F32).reshape(256, 128))
        return 0

    fetch[0].wait()
    lax.fori_loop(0, half, count_slot, 0)
    fetch[1].wait()
    fetch[2].wait()
    for c in early:
        c.start()
    lax.fori_loop(half, SLOTS, count_slot, 0)
    slot_rows = grouped_sums([s_ref[f] for f in range(4)])
    for f, r in enumerate(slot_rows):
        gift[f, 0:MOVED] = r[OWN:SLOTS]
        gift[f, MOVED : 2 * MOVED] = r[SLOTS + OWN : 2 * SLOTS]
    pl.semaphore_wait(barrier, n - me)
    gift_copy = swap(gift, given, 8)
    gift_copy.start()
    move_copies = [swap(act_ref.at[:, OWN + i], moved.at[:, i], 2 + i) for i in range(MOVED)]
    for c in move_copies:
        c.start()
    gift_copy.wait()
    rows1 = []
    for f, r in enumerate(slot_rows):
        g = given[f]
        kept = jnp.concatenate([r[0:OWN], r[SLOTS : SLOTS + OWN]], axis=0)
        mixed = jnp.concatenate([r[0:half], g[0:MOVED], r[SLOTS : SLOTS + half], g[MOVED : 2 * MOVED]], axis=0)
        rows1.append(jnp.where(heavy, kept, mixed))
    mine1[...] = packed(rows1)
    share(mine1, got1, send1, recv1)
    def row_ids(slots):
        v = jnp.full((1, 128), -1, jnp.int32)
        for j, slot in enumerate(slots):
            v = jnp.where(lane // 16 == j, jnp.where(slot < count, ids_ref[slot], -1), v)
        return v

    info[0:1] = row_ids(range(OWN))
    info[1:2] = row_ids(list(range(half)) + list(range(OWN, OWN + MOVED)))
    info[2:8] = jnp.full((6, 128), count, jnp.int32)
    info_copy = swap(info, rinfo, 0)
    info_copy.start()
    for c in late:
        c.start()
    for c in early:
        c.wait()
    for i in range(MOVED):
        move_copies[i].wait()

    def choose(i, _):
        for f in range(4):
            v = jnp.where(
                heavy, x[f, half + i].astype(F32).reshape(256, 128), moved[f, i].astype(F32).reshape(256, 128)
            )
            x[f, half + i] = v.astype(BF16).reshape(x.shape[2:])
        return 0

    lax.fori_loop(0, MOVED, choose, 0)

    def sum_of(*refs):
        total = refs[0].astype(F32)
        for r in refs[1:]:
            total = total + r.astype(F32)
        return total.astype(BF16)

    @pl.when(me == 0)
    def _():
        for b in range(3):
            k0, k1, k2 = wn[b, top, first], ws[b, top, second], ws[b, top, first]
            wa[b, top, first] = sum_of(k0, k1, k2)
            wa[b, top, second] = sum_of(k0, k1)
            wda[b, top, first] = sum_of(wd[b, top, first], wd[b, top, second], wd[b, low, second])

    norms(rows1, mine1, got1, send1, recv1, gain1_ref, shift1_ref, per_frame, p1)

    def prep(i, tiles):
        for t in range(2):
            j = 2 * i + t
            rows = slice(16 + t * 272, 272 + t * 272)
            for q in range(4):
                v = x[q, j].astype(F32).reshape(256, 128)
                h = silu_of_half(v * p1[q, 0, pl.ds(j, 1), :] + p1[q, 1, pl.ds(j, 1), :])
                left, right = shifted(h, 16)
                k = (q % 2) * 384
                tiles[q // 2, rows, k : k + 128] = left.astype(BF16)
                tiles[q // 2, rows, k + 128 : k + 256] = h.astype(BF16)
                tiles[q // 2, rows, k + 256 : k + 384] = right.astype(BF16)

    def conv(tiles, terms):
        acc = jnp.zeros((512, 256), F32)
        for p, w in terms:
            for b in range(3):
                r = b * 16
                pair = jnp.concatenate([tiles[p, r : r + 256, :], tiles[p, r + 272 : r + 528, :]], axis=0)
                acc = acc + jnp.dot(pair, w[b], preferred_element_type=F32)
        return acc

    def build(i, z, which, acc, frame):
        col = lax.broadcasted_iota(jnp.int32, (256, 128), 0) % 8
        rows = pl.ds(pl.multiple_of(i * 128, 128), 128)
        for e in range(2):
            for t in range(2):
                v = acc[t * 256 : t * 256 + 256, e * 128 : e * 128 + 128]
                if frame is not None:
                    v = v + x[frame + e, 2 * i + t].astype(F32).reshape(256, 128)
                sf[z, which, e, t * 256 : t * 256 + 256] = v
        for e in range(2):
            even = sf[z, which, e, pl.ds(0, 256, stride=2), :]
            odd = sf[z, which, e, pl.ds(1, 256, stride=2), :]
            prev = jnp.where(col == 0, 0.0, pltpu.roll(odd, 1, axis=0))
            for c, v in enumerate((prev, even, odd)):
                v = v.reshape(2, 8, 2, 8, 128)
                up_rows, low_rows = v[:, :, 0], v[:, :, 1]
                above = jnp.concatenate([jnp.zeros((2, 1, 8, 128), F32), low_rows[:, :7]], axis=1)
                k = e * 384 + c * 128
                for b, u in enumerate((above, up_rows, low_rows)):
                    lhs[which, b, rows, k : k + 128] = u.reshape(128, 128).astype(BF16)

    pairs = OWN // 2

    def part_copy(i):
        return remote(next1.at[i], part1.at[i], psend.at[i], precv.at[i], {"tm": me + 1})

    def step(i, _):
        def onward(pair, z, tiles):
            build(pair, z, 2, conv(tiles, ((1, wn),)), None)
            build(pair, z, 1, conv(tiles, ((1, ws), (0, wn))), 2)

        prep(2 * i + 1, bufo.at[i])
        onward(2 * i, 0, bufe.at[i])
        prep(jnp.minimum(2 * i + 2, pairs - 1), bufe.at[i + 1])
        onward(2 * i + 1, 1, bufo.at[i])
        rows = pl.ds(pl.multiple_of(i * 256, 256), 256)

        @pl.when(me < n)
        def _():
            both = [jnp.concatenate([lhs[1, b, rows, :], lhs[2, b, rows, :]], axis=0) for b in range(3)]
            out = dot(both[0], wd[0]) + dot(both[1], wd[1]) + dot(both[2], wd[2])
            outd[1, rows, :] = out[0:256]
            outd[2, rows, :] = out[256:512]

        next1[i, 0] = (outd[1, rows, second] + outd[2, rows, first]).astype(SENT1)
        next1[i, 1] = outd[2, rows, second].astype(SENT1)

        @pl.when(me < n - 1)
        def _():
            part_copy(i).start()

        return 0

    prep(0, bufe.at[0])
    lax.fori_loop(0, 2, step, 0)

    def own_step(i, _):
        build(2 * i, 0, 0, conv(bufe.at[i], ((0, wa),)), 0)
        build(2 * i + 1, 1, 0, conv(bufo.at[i], ((0, wa),)), 0)
        return 0

    lax.fori_loop(0, 2, own_step, 0)
    outd[0] = dot(lhs[0, 0], wda[0]) + dot(lhs[0, 1], wda[1]) + dot(lhs[0, 2], wda[2])
    for i in range(2):

        @pl.when(me > 0)
        def _():
            part_copy(i).wait_recv()

        rows = slice(i * 256, i * 256 + 256)
        for f in range(2):
            v = outd[0, rows, f * 128 : f * 128 + 128]
            if f == 1:
                v = v + outd[1, rows, first]
            v = v + part1[i, f].astype(F32)
            level[rows, f * 128 : f * 128 + 128] = v.astype(BF16)
    sums2 = []
    for f in range(2):
        v = level[:, f * 128 : f * 128 + 128].astype(F32).reshape(OWN, 64, 128)
        sums2.append(jnp.concatenate([jnp.sum(v, axis=1), jnp.sum(v * v, axis=1)], axis=0))
    rows2 = grouped_sums(sums2)
    mine2[...] = packed(rows2)
    share(mine2, got2, send2, recv2)
    for c in late:
        c.wait()
    planes[...] = jnp.dot(plane[...], level[...], preferred_element_type=F32).astype(BF16)

    @pl.when(me == 0)
    def _():
        conv2a[0] = sum_of(conv2[0], conv2[1], conv2[2])
        conv2a[1] = sum_of(conv2[0], conv2[1])
        for i in range(9):
            down2a[i] = sum_of(down2[0, i], down2[1, i], down2[2, i])

    norms(rows2, mine2, got2, send2, recv2, gain2_ref, shift2_ref, per_frame / 4, p2)

    row = lax.broadcasted_iota(jnp.int32, (128, 128), 0)

    def back_y(v, row):
        return jnp.where(row % 16 < 4, 0.0, pltpu.roll(v, 4, axis=0))

    def back_x(v, row):
        return jnp.where(row % 4 < 1, 0.0, pltpu.roll(v, 1, axis=0))

    def on_y(v, row):
        return jnp.where(row % 16 >= 12, 0.0, pltpu.roll(v, 124, axis=0))

    def on_x(v, row):
        return jnp.where(row % 4 >= 3, 0.0, pltpu.roll(v, 127, axis=0))

    for f in range(2):
        scale = p2[f, 0].reshape(OWN, 1, 128)
        bias = p2[f, 1].reshape(OWN, 1, 128)
        for yp in range(2):
            for xp in range(2):
                q = yp * 2 + xp
                v = planes[q * 128 : q * 128 + 128, f * 128 : f * 128 + 128].astype(F32)
                h = silu_of_half(v.reshape(OWN, 16, 128) * scale + bias).reshape(128, 128)
                hy = (back_y if yp else on_y)(h, row)
                move_x = back_x if xp else on_x
                for s, u in enumerate((h, move_x(h, row), hy, move_x(hy, row))):
                    blocks[f, q * 4 + s] = u.astype(BF16)

    taps = (((1, 1), (0, 0), (1, 0)), ((0, 0), (1, 0), (0, 1)))

    def gathered(f):
        rows = []
        for yp in range(2):
            for xp in range(2):
                cells = []
                for b in range(3):
                    for c in range(3):
                        (py, sy), (px, sx) = taps[yp][b], taps[xp][c]
                        cells.append(blocks[f, (py * 2 + px) * 4 + sy * 2 + sx])
                rows.append(jnp.concatenate(cells, axis=1))
        return jnp.concatenate(rows, axis=0)

    row2 = lax.broadcasted_iota(jnp.int32, (128, 256), 0)

    def spread(which, acc):
        u = [acc[q * 128 : q * 128 + 128] for q in range(4)]
        u1x, u3x, u2y, u3y = back_x(u[1], row2), back_x(u[3], row2), back_y(u[2], row2), back_y(u[3], row2)
        u3yx = back_x(u3y, row2)
        for i, v in enumerate((u3yx, u2y, u3y, u1x, u[0], u[1], u3x, u[2], u[3])):
            ublocks[which, i] = v.astype(BF16)

    spread(3, dot(gathered(1), conv2[0]))
    spread(2, dot(gathered(0), conv2[0]) + dot(gathered(1), conv2[1]))

    def down_sum(terms):
        acc = jnp.zeros((128, 256), F32)
        for which, w in terms:
            for i in range(9):
                acc = acc + dot(ublocks[which, i], w[i])
        return acc

    skip_copy = remote(next2.at[1], part2.at[1], sems.at[12], sems.at[13], {"tm": me + 2})
    next_copy = remote(next2.at[0], part2.at[0], sems.at[14], sems.at[15], {"tm": me + 1})

    @pl.when(me < n - 2)
    def _():
        next2[1] = down_sum(((2, down2.at[0]), (3, down2.at[1]))).astype(SENT2)
        skip_copy.start()

    spread(1, dot(gathered(0), conv2a[1]) + dot(gathered(1), conv2[2]) + dot(planes[:, second], short[...]))
    spread(0, dot(gathered(0), conv2a[0]) + dot(planes[:, first], short[...]))

    @pl.when(me < n - 1)
    def _():
        next2[0] = down_sum(((0, down2.at[0]), (1, down2.at[1]), (2, down2.at[2]))).astype(SENT2)
        next_copy.start()

    own = down_sum(((0, down2a),))
    info_copy.wait()
    low_lane = lane < half * 16
    its_heavy = rinfo[2:3, :] == cap
    my_ids = jnp.where(low_lane | heavy, info[0:1, :], rinfo[1:2, :])
    its_ids = jnp.where(low_lane | its_heavy, rinfo[0:1, :], info[1:2, :])
    wanted = lax.axis_index("tile") * OWN + row // 16
    cell = row % 16 == lax.broadcasted_iota(jnp.int32, (128, 128), 1) % 16
    mine = jnp.where((wanted == my_ids) & cell, 1.0, 0.0).astype(BF16)
    its = jnp.where((wanted == its_ids) & cell, 1.0, 0.0).astype(BF16)

    @pl.when(me > 1)
    def _():
        skip_copy.wait_recv()

    @pl.when(me > 0)
    def _():
        next_copy.wait_recv()

    enc[...] = (own + part2[1].astype(F32) + part2[0].astype(F32)).astype(BF16)
    enc_copy = swap(enc, renc, 1)
    enc_copy.start()
    kept = dot(mine, enc[...])
    shared(mine1, got1, send1, recv1)
    shared(mine2, got2, send2, recv2)

    @pl.when(me < n - 1)
    def _():
        for i in range(2):
            part_copy(i).wait_send()
        next_copy.wait_send()

    @pl.when(me < n - 2)
    def _():
        skip_copy.wait_send()

    enc_copy.wait()
    out_ref[...] = (kept + dot(its, renc[...])).astype(BF16).reshape(out_ref.shape)


def encode(acts, ids, counts, params, n):
    (
        first_gain,
        first_shift,
        first_conv,
        first_down,
        second_gain,
        second_shift,
        second_conv,
        second_short,
        second_down,
    ) = params
    cells = acts.shape[2:]
    rows = OWN * 64
    vm = pltpu.VMEM
    line = lambda v: v.reshape(1, 128)
    return pl.pallas_call(
        functools.partial(main_kernel, n, float(cells[0] * cells[1] * (cells[2] // GROUPS))),
        out_shape=jax.ShapeDtypeStruct((OWN * 4, 4, 256), BF16),
        in_specs=[ANY, SMEM, SMEM, VMEM, VMEM, ANY, ANY, VMEM, VMEM, ANY, ANY, ANY, ANY],
        out_specs=VMEM,
        scratch_shapes=[
            vm((4, SLOTS) + cells, BF16),
            vm((4, MOVED) + cells, BF16),
            vm((4, 2 * MOVED, 128), F32),
            vm((4, 2 * MOVED, 128), F32),
            vm((8, 128), jnp.int32),
            vm((8, 128), jnp.int32),
            vm((4, 2 * SLOTS, 128), F32),
            vm((3, 1152, 256), BF16),
            vm((2, 1152, 256), BF16),
            vm((128, 256), BF16),
            vm((3, 9, 256, 256), BF16),
            vm((9, 256, 256), BF16),
            vm((rows, rows), BF16),
            vm((4, 128), F32),
            vm((n, 4, 128), F32),
            vm((4, 128), F32),
            vm((n, 4, 128), F32),
            vm((4, 2, OWN, 128), F32),
            vm((2, 2, OWN, 128), F32),
            vm((3, 2, 560, 768), BF16),
            vm((2, 2, 560, 768), BF16),
            vm((3, 768, 256), BF16),
            vm((3, 768, 256), BF16),
            vm((3, 768, 256), BF16),
            vm((3, 768, 256), BF16),
            vm((3, 768, 256), BF16),
            vm((2, 3, 2, 512, 128), F32),
            vm((3, 3, rows, 768), BF16),
            vm((3, rows, 256), F32),
            vm((2, 2, 256, 128), SENT1),
            vm((2, 2, 256, 128), SENT1),
            vm((rows, 256), BF16),
            vm((rows, 256), BF16),
            vm((2, 16, 128, 128), BF16),
            vm((4, 9, 128, 256), BF16),
            vm((2, OWN * 16, 256), SENT2),
            vm((2, OWN * 16, 256), SENT2),
            vm((OWN * 16, 256), BF16),
            vm((OWN * 16, 256), BF16),
            pltpu.SemaphoreType.DMA((n,)),
            pltpu.SemaphoreType.DMA((n,)),
            pltpu.SemaphoreType.DMA((n,)),
            pltpu.SemaphoreType.DMA((n,)),
            pltpu.SemaphoreType.DMA((2,)),
            pltpu.SemaphoreType.DMA((2,)),
            pltpu.SemaphoreType.DMA((18,)),
            pltpu.SemaphoreType.DMA((25,)),
        ],
        name="encode",
        compiler_params=pltpu.CompilerParams(collective_id=0, has_side_effects=True, vmem_limit_bytes=LIMIT),
    )(
        acts,
        ids,
        counts,
        line(first_gain),
        line(first_shift),
        first_conv.reshape(3, 3, 384, 128),
        first_down.reshape(3, 3, 384, 128),
        line(second_gain),
        line(second_shift),
        second_conv.reshape(3, 1152, 256),
        second_short,
        second_down.reshape(3, 9, 256, 256),
        jnp.asarray(plane_matrix(), BF16),
    )


def body(activations, tile_ids, tile_counts, *params):
    n = lax.axis_size("tm")
    latents = encode(activations, tile_ids, tile_counts, params, n)
    return latents.reshape(1, OWN, 4, 4, 256)


def solution(mesh):
    placed = (
        P(("groups", "tm"), "tile", None, None, None),
        P(("groups", "tile")),
        P(("groups", "tile")),
    ) + (P(),) * 9
    return jax.shard_map(
        body,
        mesh=mesh,
        in_specs=placed,
        out_specs=P(("groups", "tm"), "tile", None, None, None),
        check_vma=False,
    )
```

```python
import functools

import jax
import jax.numpy as jnp
import numpy as np
from jax import lax
from jax.experimental import pallas as pl
from jax.experimental.pallas import tpu as pltpu
from jax.sharding import PartitionSpec as P

GROUPS = 32
OWN = 8
MOVED = 4
SLOTS = OWN + MOVED
HALF = OWN // 2
EPS = 1e-06
F32 = jnp.float32
BF16 = jnp.bfloat16
SENT1 = jnp.bfloat16
SENT2 = jnp.bfloat16
MESH = pl.DeviceIdType.MESH
VMEM = pl.BlockSpec(memory_space=pltpu.VMEM)
SMEM = pl.BlockSpec(memory_space=pltpu.SMEM)
ANY = pl.BlockSpec(memory_space=pl.ANY)
LIMIT = 56 << 20


def silu_of_half(w):
    return w + w * jnp.tanh(w)


def dot(a, b):
    return jnp.dot(a, b, preferred_element_type=F32)


def shifted(v, side):
    rows = v.shape[0]
    col = lax.broadcasted_iota(jnp.int32, v.shape, 0) % side
    left = jnp.where(col == 0, 0.0, pltpu.roll(v, 1, axis=0))
    right = jnp.where(col == side - 1, 0.0, pltpu.roll(v, rows - 1, axis=0))
    return left, right


def plane_matrix():
    m = np.zeros((2, 2, HALF, 4, 4, HALF, 8, 8), np.float32)
    for yp in range(2):
        for xp in range(2):
            for t in range(HALF):
                for y in range(4):
                    for x in range(4):
                        m[yp, xp, t, y, x, t, 2 * y + yp, 2 * x + xp] = 1.0
    return m.reshape(HALF * 64, HALF * 64)


def main_kernel(
    n,
    per_frame,
    act_ref,
    ids_ref,
    count_ref,
    gain1_ref,
    shift1_ref,
    conv1_hbm,
    down1_hbm,
    gain2_ref,
    shift2_ref,
    conv2_hbm,
    short_hbm,
    down2_hbm,
    plane_hbm,
    out_ref,
    x,
    moved,
    gift,
    given,
    info,
    rinfo,
    s_ref,
    conv2,
    conv2a,
    short,
    down2,
    down2a,
    plane,
    mine1,
    got1,
    mine2,
    got2,
    p1,
    p2,
    bufe,
    bufo,
    ws,
    wn,
    wa,
    wd,
    wda,
    sf,
    lhs,
    outd,
    next1,
    part1,
    level,
    planes,
    blocks,
    ublocks,
    next2,
    part2,
    enc,
    renc,
    send1,
    recv1,
    send2,
    recv2,
    send3,
    recv3,
    psend,
    precv,
    sems,
    local,
):
    me = lax.axis_index("tm")
    partner = 1 - lax.axis_index("tile")
    cap = act_ref.shape[1]
    used = [0]

    def copy_in(src, dst):
        c = pltpu.make_async_copy(src, dst, local.at[used[0]])
        used[0] += 1
        return c

    half = OWN - MOVED
    fetch = [
        copy_in(act_ref.at[:, 0:half], x.at[:, 0:half]),
        copy_in(act_ref.at[:, half:OWN], x.at[:, half:OWN]),
        copy_in(act_ref.at[:, OWN : OWN + MOVED], x.at[:, OWN : OWN + MOVED]),
    ]
    for c in fetch:
        c.start()
    barrier = pltpu.get_barrier_semaphore()
    pl.semaphore_signal(barrier, inc=1, device_id={"tile": partner}, device_id_type=MESH)

    def greet(k, _):
        pl.semaphore_signal(barrier, inc=1, device_id={"tm": me - k}, device_id_type=MESH)
        return 0

    lax.fori_loop(1, me + 1, greet, 0)

    lane = lax.broadcasted_iota(jnp.int32, (1, 128), 1)
    count = count_ref[0]
    heavy = jnp.full((1, 128), count, jnp.int32) == cap

    def remote(src, dst, send_sem, recv_sem, target):
        return pltpu.make_async_remote_copy(
            src_ref=src, dst_ref=dst, send_sem=send_sem, recv_sem=recv_sem, device_id=target, device_id_type=MESH
        )

    def swap(src, dst, i):
        return remote(src, dst, sems.at[2 * i], sems.at[2 * i + 1], {"tile": partner})

    def quarter(rows):
        return lax.broadcasted_iota(jnp.int32, (rows, 128), 1) % 4

    def grouped_sums(sums):
        ri = lax.broadcasted_iota(jnp.int32, (128, 128), 0) // (128 // GROUPS)
        ci = lax.broadcasted_iota(jnp.int32, (128, 128), 1) // (128 // GROUPS)
        same = jnp.where(ri == ci, 1.0, 0.0).astype(F32)
        rows = jnp.dot(
            jnp.concatenate(sums, axis=0), same, precision=lax.Precision.HIGHEST, preferred_element_type=F32
        )
        size = sums[0].shape[0]
        return [rows[f * size : (f + 1) * size] for f in range(len(sums))]

    def packed(rows):
        total = rows[0]
        for r in rows[1:]:
            total = total + r
        k = total.shape[0] // 4
        v = total[0:k]
        for q in range(1, 4):
            v = jnp.where(quarter(k) == q, total[k * q : k * q + k], v)
        return v

    def unpacked(v):
        at = quarter(v.shape[0])
        parts = [jnp.where(at == 0, v, 0.0)]
        for q in range(1, 4):
            parts.append(pltpu.roll(jnp.where(at == q, v, 0.0), 128 - q, axis=1))
        w = jnp.concatenate(parts, axis=0)
        w = w + pltpu.roll(w, 1, axis=1)
        return w + pltpu.roll(w, 2, axis=1)

    top, low = slice(0, 384), slice(384, 768)
    first, second = slice(0, 128), slice(128, 256)

    def sum_copy(mine, got, sent, here, k):
        return remote(mine, got.at[k], sent.at[k], here.at[k], {"tm": me + k})

    def share(mine, got, sent, here):
        def start(i, _):
            sum_copy(mine, got, sent, here, n - me - i).start()
            return 0

        lax.fori_loop(1, n - me, start, 0)

    def shared(mine, got, sent, here):
        def wait(k, _):
            sum_copy(mine, got, sent, here, k).wait_send()
            return 0

        lax.fori_loop(1, n - me, wait, 0)

    def norms(rows, mine, got, sent, here, gain, shift, size, out):
        def take(k, run):
            sum_copy(mine, got, sent, here, k).wait_recv()
            return run + got[k]

        run = unpacked(lax.fori_loop(1, me + 1, take, jnp.zeros(mine.shape, F32)))
        tiles = rows[0].shape[0] // 2
        start = (me * len(rows)).astype(F32)
        for i, r in enumerate(rows):
            run = run + r
            inv_count = jnp.full((1, 128), 1.0, F32) / (jnp.zeros((1, 128), F32) + (start + float(i + 1)) * size)
            m = run[0:tiles] * inv_count
            var = run[tiles : 2 * tiles] * inv_count - m * m
            scale = lax.rsqrt(var + EPS) * gain[...]
            out[i, 0] = 0.5 * scale
            out[i, 1] = 0.5 * (shift[...] - m * scale)

    zero = jnp.zeros((384, 128), BF16)
    for b in range(3):
        ws[b, 384:768, 0:128] = zero
        wa[b, 384:768, 0:128] = zero
        wn[b, 0:384, 128:256] = zero
        wd[b, 384:768, 0:128] = zero
        wda[b, 384:768, 0:128] = zero
    edge = jnp.zeros((16, 768), BF16)
    for tiles in (bufe, bufo):
        for i in range(2):
            for p in range(2):
                for r in (0, 272, 544):
                    tiles[i, p, r : r + 16] = edge


    @pl.when(me == 0)
    def _():
        part1[...] = jnp.zeros_like(part1)
        part2[...] = jnp.zeros_like(part2)

    @pl.when(me == 1)
    def _():
        part2[1] = jnp.zeros_like(part2[1])

    early = [
        copy_in(h.at[a], w.at[:, r, c])
        for h, a, w, r, c in (
            (conv1_hbm, 0, wn, top, first),
            (conv1_hbm, 1, wn, low, first),
            (conv1_hbm, 0, wn, low, second),
            (conv1_hbm, 2, ws, top, first),
            (conv1_hbm, 1, ws, top, second),
            (conv1_hbm, 2, ws, low, second),
            (conv1_hbm, 2, wa, top, first),
            (conv1_hbm, 1, wa, top, second),
            (conv1_hbm, 2, wa, low, second),
            (down1_hbm, 2, wd, top, first),
            (down1_hbm, 0, wd, top, second),
            (down1_hbm, 1, wd, low, second),
            (down1_hbm, 2, wda, top, first),
            (down1_hbm, 0, wda, top, second),
            (down1_hbm, 1, wda, low, second),
        )
    ]
    late = [
        copy_in(a, b)
        for a, b in (
            (plane_hbm, plane),
            (conv2_hbm, conv2),
            (conv2_hbm.at[2], conv2a.at[0]),
            (conv2_hbm.at[1], conv2a.at[1]),
            (short_hbm, short),
            (down2_hbm, down2),
            (down2_hbm.at[2], down2a),
        )
    ]

    def add_up(f, j, v):
        s_ref[f, pl.ds(j, 1), :] = jnp.sum(v, axis=0, keepdims=True)
        s_ref[f, pl.ds(SLOTS + j, 1), :] = jnp.sum(v * v, axis=0, keepdims=True)

    def count_slot(j, _):
        for f in range(4):
            add_up(f, j, x[f, j].astype(F32).reshape(256, 128))
        return 0

    fetch[0].wait()
    lax.fori_loop(0, half, count_slot, 0)
    fetch[1].wait()
    fetch[2].wait()
    for c in early:
        c.start()
    lax.fori_loop(half, SLOTS, count_slot, 0)
    slot_rows = grouped_sums([s_ref[f] for f in range(4)])
    for f, r in enumerate(slot_rows):
        gift[f, 0:MOVED] = r[OWN:SLOTS]
        gift[f, MOVED : 2 * MOVED] = r[SLOTS + OWN : 2 * SLOTS]
    pl.semaphore_wait(barrier, n - me)
    gift_copy = swap(gift, given, 8)
    gift_copy.start()
    move_copies = [swap(act_ref.at[:, OWN + i], moved.at[:, i], 2 + i) for i in range(MOVED)]
    for c in move_copies:
        c.start()
    gift_copy.wait()
    rows1 = []
    for f, r in enumerate(slot_rows):
        g = given[f]
        kept = jnp.concatenate([r[0:OWN], r[SLOTS : SLOTS + OWN]], axis=0)
        mixed = jnp.concatenate([r[0:half], g[0:MOVED], r[SLOTS : SLOTS + half], g[MOVED : 2 * MOVED]], axis=0)
        rows1.append(jnp.where(heavy, kept, mixed))
    mine1[...] = packed(rows1)
    share(mine1, got1, send1, recv1)
    def row_ids(slots):
        v = jnp.full((1, 128), -1, jnp.int32)
        for j, slot in enumerate(slots):
            v = jnp.where(lane // 16 == j, jnp.where(slot < count, ids_ref[slot], -1), v)
        return v

    info[0:1] = row_ids(range(OWN))
    info[1:2] = row_ids(list(range(half)) + list(range(OWN, OWN + MOVED)))
    info[2:8] = jnp.full((6, 128), count, jnp.int32)
    info_copy = swap(info, rinfo, 0)
    info_copy.start()
    for c in late:
        c.start()
    for c in early:
        c.wait()
    for i in range(MOVED):
        move_copies[i].wait()

    def choose(i, _):
        for f in range(4):
            v = jnp.where(
                heavy, x[f, half + i].astype(F32).reshape(256, 128), moved[f, i].astype(F32).reshape(256, 128)
            )
            x[f, half + i] = v.astype(BF16).reshape(x.shape[2:])
        return 0

    lax.fori_loop(0, MOVED, choose, 0)

    def sum_of(*refs):
        total = refs[0].astype(F32)
        for r in refs[1:]:
            total = total + r.astype(F32)
        return total.astype(BF16)

    @pl.when(me == 0)
    def _():
        for b in range(3):
            k0, k1, k2 = wn[b, top, first], ws[b, top, second], ws[b, top, first]
            wa[b, top, first] = sum_of(k0, k1, k2)
            wa[b, top, second] = sum_of(k0, k1)
            wda[b, top, first] = sum_of(wd[b, top, first], wd[b, top, second], wd[b, low, second])

    norms(rows1, mine1, got1, send1, recv1, gain1_ref, shift1_ref, per_frame, p1)

    def prep(i, tiles):
        for t in range(2):
            j = 2 * i + t
            rows = slice(16 + t * 272, 272 + t * 272)
            for q in range(4):
                v = x[q, j].astype(F32).reshape(256, 128)
                h = silu_of_half(v * p1[q, 0, pl.ds(j, 1), :] + p1[q, 1, pl.ds(j, 1), :])
                left, right = shifted(h, 16)
                k = (q % 2) * 384
                tiles[q // 2, rows, k : k + 128] = left.astype(BF16)
                tiles[q // 2, rows, k + 128 : k + 256] = h.astype(BF16)
                tiles[q // 2, rows, k + 256 : k + 384] = right.astype(BF16)

    def conv(tiles, terms):
        acc = jnp.zeros((512, 256), F32)
        for p, w in terms:
            for b in range(3):
                r = b * 16
                pair = jnp.concatenate([tiles[p, r : r + 256, :], tiles[p, r + 272 : r + 528, :]], axis=0)
                acc = acc + jnp.dot(pair, w[b], preferred_element_type=F32)
        return acc

    def build(i, z, which, acc, frame):
        col = lax.broadcasted_iota(jnp.int32, (256, 128), 0) % 8
        rows = pl.ds(pl.multiple_of(i * 128, 128), 128)
        for e in range(2):
            for t in range(2):
                v = acc[t * 256 : t * 256 + 256, e * 128 : e * 128 + 128]
                if frame is not None:
                    v = v + x[frame + e, 2 * i + t].astype(F32).reshape(256, 128)
                sf[z, which, e, t * 256 : t * 256 + 256] = v
        for e in range(2):
            even = sf[z, which, e, pl.ds(0, 256, stride=2), :]
            odd = sf[z, which, e, pl.ds(1, 256, stride=2), :]
            prev = jnp.where(col == 0, 0.0, pltpu.roll(odd, 1, axis=0))
            for c, v in enumerate((prev, even, odd)):
                v = v.reshape(2, 8, 2, 8, 128)
                up_rows, low_rows = v[:, :, 0], v[:, :, 1]
                above = jnp.concatenate([jnp.zeros((2, 1, 8, 128), F32), low_rows[:, :7]], axis=1)
                k = e * 384 + c * 128
                for b, u in enumerate((above, up_rows, low_rows)):
                    lhs[which, b, rows, k : k + 128] = u.reshape(128, 128).astype(BF16)

    pairs = OWN // 2

    def part_copy(i):
        return remote(next1.at[i], part1.at[i], psend.at[i], precv.at[i], {"tm": me + 1})

    def step(i, _):
        def onward(pair, z, tiles):
            build(pair, z, 2, conv(tiles, ((1, wn),)), None)
            build(pair, z, 1, conv(tiles, ((1, ws), (0, wn))), 2)

        prep(2 * i + 1, bufo.at[i])
        onward(2 * i, 0, bufe.at[i])
        prep(jnp.minimum(2 * i + 2, pairs - 1), bufe.at[i + 1])
        onward(2 * i + 1, 1, bufo.at[i])
        rows = pl.ds(pl.multiple_of(i * 256, 256), 256)

        @pl.when(me < n)
        def _():
            both = [jnp.concatenate([lhs[1, b, rows, :], lhs[2, b, rows, :]], axis=0) for b in range(3)]
            out = dot(both[0], wd[0]) + dot(both[1], wd[1]) + dot(both[2], wd[2])
            outd[1, rows, :] = out[0:256]
            outd[2, rows, :] = out[256:512]

        next1[i, 0] = (outd[1, rows, second] + outd[2, rows, first]).astype(SENT1)
        next1[i, 1] = outd[2, rows, second].astype(SENT1)

        @pl.when(me < n - 1)
        def _():
            part_copy(i).start()

        return 0

    prep(0, bufe.at[0])
    lax.fori_loop(0, 2, step, 0)

    sums2 = (send2, recv2), (send3, recv3)
    rows2 = []
    for i in range(2):
        rows = slice(i * 256, i * 256 + 256)
        build(2 * i, 0, 0, conv(bufe.at[i], ((0, wa),)), 0)
        build(2 * i + 1, 1, 0, conv(bufo.at[i], ((0, wa),)), 0)

        @pl.when(me < n)
        def _():
            outd[0, rows, :] = (
                dot(lhs[0, 0, rows, :], wda[0]) + dot(lhs[0, 1, rows, :], wda[1]) + dot(lhs[0, 2, rows, :], wda[2])
            )

        @pl.when(me > 0)
        def _():
            part_copy(i).wait_recv()

        totals = []
        for f in range(2):
            v = outd[0, rows, f * 128 : f * 128 + 128]
            if f == 1:
                v = v + outd[1, rows, first]
            v = (v + part1[i, f].astype(F32)).astype(BF16)
            level[rows, f * 128 : f * 128 + 128] = v
            v = v.astype(F32).reshape(HALF, 64, 128)
            totals.append(jnp.concatenate([jnp.sum(v, axis=1), jnp.sum(v * v, axis=1)], axis=0))
        rows2.append(grouped_sums(totals))
        mine2[i] = packed(rows2[i])
        share(mine2.at[i], got2.at[i], *sums2[i])
    for c in late:
        c.wait()
    for i in range(2):
        rows = slice(i * 256, i * 256 + 256)
        planes[rows, :] = dot(plane[...], level[rows, :]).astype(BF16)

    @pl.when(me == 0)
    def _():
        conv2a[0] = sum_of(conv2[0], conv2[1], conv2[2])
        conv2a[1] = sum_of(conv2[0], conv2[1])
        for i in range(9):
            down2a[i] = sum_of(down2[0, i], down2[1, i], down2[2, i])

    row = lax.broadcasted_iota(jnp.int32, (128, 128), 0)

    def back_y(v, row):
        return jnp.where(row % 16 < 4, 0.0, pltpu.roll(v, 4, axis=0))

    def back_x(v, row):
        return jnp.where(row % 4 < 1, 0.0, pltpu.roll(v, 1, axis=0))

    def on_y(v, row):
        return jnp.where(row % 16 >= 12, 0.0, pltpu.roll(v, v.shape[0] - 4, axis=0))

    def on_x(v, row):
        return jnp.where(row % 4 >= 3, 0.0, pltpu.roll(v, v.shape[0] - 1, axis=0))

    def second_hidden(h):
        norms(rows2[h], mine2.at[h], got2.at[h], *sums2[h], gain2_ref, shift2_ref, per_frame / 4, p2.at[h])
        here = row[0:64]
        for f in range(2):
            scale = p2[h, f, 0].reshape(HALF, 1, 128)
            bias = p2[h, f, 1].reshape(HALF, 1, 128)
            for yp in range(2):
                for xp in range(2):
                    q = yp * 2 + xp
                    r = h * 256 + q * 64
                    v = planes[r : r + 64, f * 128 : f * 128 + 128].astype(F32)
                    v = silu_of_half(v.reshape(HALF, 16, 128) * scale + bias).reshape(64, 128)
                    vy = (back_y if yp else on_y)(v, here)
                    move_x = back_x if xp else on_x
                    for k, u in enumerate((v, move_x(v, here), vy, move_x(vy, here))):
                        blocks[f, q * 4 + k, h * 64 : h * 64 + 64] = u.astype(BF16)

    taps = (((1, 1), (0, 0), (1, 0)), ((0, 0), (1, 0), (0, 1)))

    def gathered(f, h):
        rows = []
        for yp in range(2):
            for xp in range(2):
                cells = []
                for b in range(3):
                    for c in range(3):
                        (py, sy), (px, sx) = taps[yp][b], taps[xp][c]
                        cells.append(blocks[f, (py * 2 + px) * 4 + sy * 2 + sx, h * 64 : h * 64 + 64])
                rows.append(jnp.concatenate(cells, axis=1))
        return jnp.concatenate(rows, axis=0)

    def wide(*parts):
        return jnp.concatenate(parts, axis=1)

    def tall(*parts):
        return jnp.concatenate(parts, axis=0)

    row2 = lax.broadcasted_iota(jnp.int32, (64, 256), 0)

    def spread(which, acc, h):
        u = [acc[q * 64 : q * 64 + 64] for q in range(4)]
        u1x, u3x, u2y, u3y = back_x(u[1], row2), back_x(u[3], row2), back_y(u[2], row2), back_y(u[3], row2)
        u3yx = back_x(u3y, row2)
        for i, v in enumerate((u3yx, u2y, u3y, u1x, u[0], u[1], u3x, u[2], u[3])):
            ublocks[which, i, h * 64 : h * 64 + 64] = v.astype(BF16)

    def onward2(h):
        spread(3, dot(gathered(1, h), conv2[0]), h)
        spread(2, dot(wide(gathered(0, h), gathered(1, h)), tall(conv2[0], conv2[1])), h)

    def own2(h):
        levels = planes[h * 256 : h * 256 + 256]
        both = wide(gathered(0, h), gathered(1, h), levels[:, second])
        spread(1, dot(both, tall(conv2a[1], conv2[2], short[...])), h)
        spread(0, dot(wide(gathered(0, h), levels[:, first]), tall(conv2a[0], short[...])), h)

    second_hidden(0)
    onward2(0)
    own2(0)
    second_hidden(1)
    onward2(1)

    def down_sum(terms):
        acc = jnp.zeros((128, 256), F32)
        for which, w in terms:
            for i in range(9):
                acc = acc + dot(ublocks[which, i], w[i])
        return acc

    skip_copy = remote(next2.at[1], part2.at[1], sems.at[12], sems.at[13], {"tm": me + 2})
    next_copy = remote(next2.at[0], part2.at[0], sems.at[14], sems.at[15], {"tm": me + 1})

    @pl.when(me < n - 2)
    def _():
        next2[1] = down_sum(((2, down2.at[0]), (3, down2.at[1]))).astype(SENT2)
        skip_copy.start()

    own2(1)

    @pl.when(me < n - 1)
    def _():
        next2[0] = down_sum(((0, down2.at[0]), (1, down2.at[1]), (2, down2.at[2]))).astype(SENT2)
        next_copy.start()

    own = down_sum(((0, down2a),))
    info_copy.wait()
    low_lane = lane < half * 16
    its_heavy = rinfo[2:3, :] == cap
    my_ids = jnp.where(low_lane | heavy, info[0:1, :], rinfo[1:2, :])
    its_ids = jnp.where(low_lane | its_heavy, rinfo[0:1, :], info[1:2, :])
    wanted = lax.axis_index("tile") * OWN + row // 16
    cell = row % 16 == lax.broadcasted_iota(jnp.int32, (128, 128), 1) % 16
    mine = jnp.where((wanted == my_ids) & cell, 1.0, 0.0).astype(BF16)
    its = jnp.where((wanted == its_ids) & cell, 1.0, 0.0).astype(BF16)

    @pl.when(me > 1)
    def _():
        skip_copy.wait_recv()

    @pl.when(me > 0)
    def _():
        next_copy.wait_recv()

    enc[...] = (own + part2[1].astype(F32) + part2[0].astype(F32)).astype(BF16)
    enc_copy = swap(enc, renc, 1)
    enc_copy.start()
    kept = dot(mine, enc[...])
    shared(mine1, got1, send1, recv1)
    for i in range(2):
        shared(mine2.at[i], got2.at[i], *sums2[i])

    @pl.when(me < n - 1)
    def _():
        for i in range(2):
            part_copy(i).wait_send()
        next_copy.wait_send()

    @pl.when(me < n - 2)
    def _():
        skip_copy.wait_send()

    enc_copy.wait()
    out_ref[...] = (kept + dot(its, renc[...])).astype(BF16).reshape(out_ref.shape)


def encode(acts, ids, counts, params, n):
    (
        first_gain,
        first_shift,
        first_conv,
        first_down,
        second_gain,
        second_shift,
        second_conv,
        second_short,
        second_down,
    ) = params
    cells = acts.shape[2:]
    rows = OWN * 64
    vm = pltpu.VMEM
    line = lambda v: v.reshape(1, 128)
    return pl.pallas_call(
        functools.partial(main_kernel, n, float(cells[0] * cells[1] * (cells[2] // GROUPS))),
        out_shape=jax.ShapeDtypeStruct((OWN * 4, 4, 256), BF16),
        in_specs=[ANY, SMEM, SMEM, VMEM, VMEM, ANY, ANY, VMEM, VMEM, ANY, ANY, ANY, ANY],
        out_specs=VMEM,
        scratch_shapes=[
            vm((4, SLOTS) + cells, BF16),
            vm((4, MOVED) + cells, BF16),
            vm((4, 2 * MOVED, 128), F32),
            vm((4, 2 * MOVED, 128), F32),
            vm((8, 128), jnp.int32),
            vm((8, 128), jnp.int32),
            vm((4, 2 * SLOTS, 128), F32),
            vm((3, 1152, 256), BF16),
            vm((2, 1152, 256), BF16),
            vm((128, 256), BF16),
            vm((3, 9, 256, 256), BF16),
            vm((9, 256, 256), BF16),
            vm((HALF * 64, HALF * 64), BF16),
            vm((4, 128), F32),
            vm((n, 4, 128), F32),
            vm((2, 2, 128), F32),
            vm((2, n, 2, 128), F32),
            vm((4, 2, OWN, 128), F32),
            vm((2, 2, 2, HALF, 128), F32),
            vm((3, 2, 560, 768), BF16),
            vm((2, 2, 560, 768), BF16),
            vm((3, 768, 256), BF16),
            vm((3, 768, 256), BF16),
            vm((3, 768, 256), BF16),
            vm((3, 768, 256), BF16),
            vm((3, 768, 256), BF16),
            vm((2, 3, 2, 512, 128), F32),
            vm((3, 3, rows, 768), BF16),
            vm((3, rows, 256), F32),
            vm((2, 2, 256, 128), SENT1),
            vm((2, 2, 256, 128), SENT1),
            vm((rows, 256), BF16),
            vm((rows, 256), BF16),
            vm((2, 16, 128, 128), BF16),
            vm((4, 9, 128, 256), BF16),
            vm((2, OWN * 16, 256), SENT2),
            vm((2, OWN * 16, 256), SENT2),
            vm((OWN * 16, 256), BF16),
            vm((OWN * 16, 256), BF16),
            pltpu.SemaphoreType.DMA((n,)),
            pltpu.SemaphoreType.DMA((n,)),
            pltpu.SemaphoreType.DMA((n,)),
            pltpu.SemaphoreType.DMA((n,)),
            pltpu.SemaphoreType.DMA((n,)),
            pltpu.SemaphoreType.DMA((n,)),
            pltpu.SemaphoreType.DMA((2,)),
            pltpu.SemaphoreType.DMA((2,)),
            pltpu.SemaphoreType.DMA((18,)),
            pltpu.SemaphoreType.DMA((25,)),
        ],
        name="encode",
        compiler_params=pltpu.CompilerParams(collective_id=0, has_side_effects=True, vmem_limit_bytes=LIMIT),
    )(
        acts,
        ids,
        counts,
        line(first_gain),
        line(first_shift),
        first_conv.reshape(3, 3, 384, 128),
        first_down.reshape(3, 3, 384, 128),
        line(second_gain),
        line(second_shift),
        second_conv.reshape(3, 1152, 256),
        second_short,
        second_down.reshape(3, 9, 256, 256),
        jnp.asarray(plane_matrix(), BF16),
    )


def body(activations, tile_ids, tile_counts, *params):
    n = lax.axis_size("tm")
    latents = encode(activations, tile_ids, tile_counts, params, n)
    return latents.reshape(1, OWN, 4, 4, 256)


def solution(mesh):
    placed = (
        P(("groups", "tm"), "tile", None, None, None),
        P(("groups", "tile")),
        P(("groups", "tile")),
    ) + (P(),) * 9
    return jax.shard_map(
        body,
        mesh=mesh,
        in_specs=placed,
        out_specs=P(("groups", "tm"), "tile", None, None, None),
        check_vma=False,
    )
```

```python
import functools

import jax
import jax.numpy as jnp
import numpy as np
from jax import lax
from jax.experimental import pallas as pl
from jax.experimental.pallas import tpu as pltpu
from jax.sharding import PartitionSpec as P

GROUPS = 32
OWN = 8
MOVED = 4
SLOTS = OWN + MOVED
HALF = OWN // 2
EPS = 1e-06
F32 = jnp.float32
BF16 = jnp.bfloat16
SENT1 = jnp.bfloat16
SENT2 = jnp.bfloat16
MESH = pl.DeviceIdType.MESH
VMEM = pl.BlockSpec(memory_space=pltpu.VMEM)
SMEM = pl.BlockSpec(memory_space=pltpu.SMEM)
ANY = pl.BlockSpec(memory_space=pl.ANY)
LIMIT = 56 << 20


def silu_of_half(w):
    return w + w * jnp.tanh(w)


def dot(a, b):
    return jnp.dot(a, b, preferred_element_type=F32)


def shifted(v, side):
    rows = v.shape[0]
    col = lax.broadcasted_iota(jnp.int32, v.shape, 0) % side
    left = jnp.where(col == 0, 0.0, pltpu.roll(v, 1, axis=0))
    right = jnp.where(col == side - 1, 0.0, pltpu.roll(v, rows - 1, axis=0))
    return left, right


def plane_matrix():
    m = np.zeros((2, 2, HALF, 4, 4, HALF, 8, 8), np.float32)
    for yp in range(2):
        for xp in range(2):
            for t in range(HALF):
                for y in range(4):
                    for x in range(4):
                        m[yp, xp, t, y, x, t, 2 * y + yp, 2 * x + xp] = 1.0
    return m.reshape(HALF * 64, HALF * 64)


def main_kernel(
    n,
    per_frame,
    act_ref,
    ids_ref,
    count_ref,
    gain1_ref,
    shift1_ref,
    conv1_hbm,
    down1_hbm,
    gain2_ref,
    shift2_ref,
    conv2_hbm,
    short_hbm,
    down2_hbm,
    plane_hbm,
    out_ref,
    x,
    moved,
    gift,
    given,
    info,
    rinfo,
    s_ref,
    conv2,
    conv2a,
    short,
    down2,
    down2a,
    plane,
    mine1,
    got1,
    mine2,
    got2,
    p1,
    p2,
    bufe,
    bufo,
    ws,
    wn,
    wa,
    wd,
    wda,
    sf,
    lhs,
    outd,
    next1,
    part1,
    level,
    planes,
    blocks,
    ublocks,
    next2,
    part2,
    enc,
    renc,
    send1,
    recv1,
    send2,
    recv2,
    send3,
    recv3,
    psend,
    precv,
    sems,
    local,
):
    me = lax.axis_index("tm")
    partner = 1 - lax.axis_index("tile")
    cap = act_ref.shape[1]
    used = [0]

    def copy_in(src, dst):
        c = pltpu.make_async_copy(src, dst, local.at[used[0]])
        used[0] += 1
        return c

    half = OWN - MOVED
    fetch = [
        copy_in(act_ref.at[:, 0:half], x.at[:, 0:half]),
        copy_in(act_ref.at[:, half:OWN], x.at[:, half:OWN]),
        copy_in(act_ref.at[:, OWN : OWN + MOVED], x.at[:, OWN : OWN + MOVED]),
    ]
    for c in fetch:
        c.start()
    barrier = pltpu.get_barrier_semaphore()
    pl.semaphore_signal(barrier, inc=1, device_id={"tile": partner}, device_id_type=MESH)

    def greet(k, _):
        pl.semaphore_signal(barrier, inc=1, device_id={"tm": me - k}, device_id_type=MESH)
        return 0

    lax.fori_loop(1, me + 1, greet, 0)

    lane = lax.broadcasted_iota(jnp.int32, (1, 128), 1)
    count = count_ref[0]
    heavy = jnp.full((1, 128), count, jnp.int32) == cap

    def remote(src, dst, send_sem, recv_sem, target):
        return pltpu.make_async_remote_copy(
            src_ref=src, dst_ref=dst, send_sem=send_sem, recv_sem=recv_sem, device_id=target, device_id_type=MESH
        )

    def swap(src, dst, i):
        return remote(src, dst, sems.at[2 * i], sems.at[2 * i + 1], {"tile": partner})

    def quarter(rows):
        return lax.broadcasted_iota(jnp.int32, (rows, 128), 1) % 4

    def grouped_sums(sums):
        ri = lax.broadcasted_iota(jnp.int32, (128, 128), 0) // (128 // GROUPS)
        ci = lax.broadcasted_iota(jnp.int32, (128, 128), 1) // (128 // GROUPS)
        same = jnp.where(ri == ci, 1.0, 0.0).astype(F32)
        rows = jnp.dot(
            jnp.concatenate(sums, axis=0), same, precision=lax.Precision.HIGHEST, preferred_element_type=F32
        )
        size = sums[0].shape[0]
        return [rows[f * size : (f + 1) * size] for f in range(len(sums))]

    def packed(rows):
        total = rows[0]
        for r in rows[1:]:
            total = total + r
        k = total.shape[0] // 4
        v = total[0:k]
        for q in range(1, 4):
            v = jnp.where(quarter(k) == q, total[k * q : k * q + k], v)
        return v

    def unpacked(v):
        at = quarter(v.shape[0])
        parts = [jnp.where(at == 0, v, 0.0)]
        for q in range(1, 4):
            parts.append(pltpu.roll(jnp.where(at == q, v, 0.0), 128 - q, axis=1))
        w = jnp.concatenate(parts, axis=0)
        w = w + pltpu.roll(w, 1, axis=1)
        return w + pltpu.roll(w, 2, axis=1)

    top, low = slice(0, 384), slice(384, 768)
    first, second = slice(0, 128), slice(128, 256)

    def sum_copy(mine, got, sent, here, k):
        return remote(mine, got.at[k], sent.at[k], here.at[k], {"tm": me + k})

    def share(mine, got, sent, here):
        def start(i, _):
            sum_copy(mine, got, sent, here, n - me - i).start()
            return 0

        lax.fori_loop(1, n - me, start, 0)

    def shared(mine, got, sent, here):
        def wait(k, _):
            sum_copy(mine, got, sent, here, k).wait_send()
            return 0

        lax.fori_loop(1, n - me, wait, 0)

    def norms(rows, mine, got, sent, here, gain, shift, size, out):
        def take(k, run):
            sum_copy(mine, got, sent, here, k).wait_recv()
            return run + got[k]

        run = unpacked(lax.fori_loop(1, me + 1, take, jnp.zeros(mine.shape, F32)))
        tiles = rows[0].shape[0] // 2
        start = (me * len(rows)).astype(F32)
        for i, r in enumerate(rows):
            run = run + r
            inv_count = jnp.full((1, 128), 1.0, F32) / (jnp.zeros((1, 128), F32) + (start + float(i + 1)) * size)
            m = run[0:tiles] * inv_count
            var = run[tiles : 2 * tiles] * inv_count - m * m
            scale = lax.rsqrt(jnp.maximum(var, 0.0) + EPS) * gain[...]
            out[i, 0] = 0.5 * scale
            out[i, 1] = 0.5 * (shift[...] - m * scale)

    zero = jnp.zeros((384, 128), BF16)
    for b in range(3):
        ws[b, 384:768, 0:128] = zero
        wa[b, 384:768, 0:128] = zero
        wn[b, 0:384, 128:256] = zero
        wd[b, 384:768, 0:128] = zero
        wda[b, 384:768, 0:128] = zero
    edge = jnp.zeros((16, 768), BF16)
    for tiles in (bufe, bufo):
        for i in range(2):
            for p in range(2):
                for r in (0, 272, 544):
                    tiles[i, p, r : r + 16] = edge


    @pl.when(me == 0)
    def _():
        part1[...] = jnp.zeros_like(part1)
        part2[...] = jnp.zeros_like(part2)

    @pl.when(me == 1)
    def _():
        part2[1] = jnp.zeros_like(part2[1])

    early = [
        copy_in(h.at[a], w.at[:, r, c])
        for h, a, w, r, c in (
            (conv1_hbm, 0, wn, top, first),
            (conv1_hbm, 1, wn, low, first),
            (conv1_hbm, 0, wn, low, second),
            (conv1_hbm, 2, ws, top, first),
            (conv1_hbm, 1, ws, top, second),
            (conv1_hbm, 2, ws, low, second),
            (conv1_hbm, 2, wa, top, first),
            (conv1_hbm, 1, wa, top, second),
            (conv1_hbm, 2, wa, low, second),
            (down1_hbm, 2, wd, top, first),
            (down1_hbm, 0, wd, top, second),
            (down1_hbm, 1, wd, low, second),
            (down1_hbm, 2, wda, top, first),
            (down1_hbm, 0, wda, top, second),
            (down1_hbm, 1, wda, low, second),
        )
    ]
    late = [
        copy_in(a, b)
        for a, b in (
            (plane_hbm, plane),
            (conv2_hbm, conv2),
            (conv2_hbm.at[2], conv2a.at[0]),
            (conv2_hbm.at[1], conv2a.at[1]),
            (short_hbm, short),
            (down2_hbm, down2),
            (down2_hbm.at[2], down2a),
        )
    ]

    def add_up(f, j, v):
        s_ref[f, pl.ds(j, 1), :] = jnp.sum(v, axis=0, keepdims=True)
        s_ref[f, pl.ds(SLOTS + j, 1), :] = jnp.sum(v * v, axis=0, keepdims=True)

    def count_slot(j, _):
        for f in range(4):
            add_up(f, j, x[f, j].astype(F32).reshape(256, 128))
        return 0

    fetch[0].wait()
    lax.fori_loop(0, half, count_slot, 0)
    fetch[1].wait()
    fetch[2].wait()
    for c in early:
        c.start()
    lax.fori_loop(half, SLOTS, count_slot, 0)
    slot_rows = grouped_sums([s_ref[f] for f in range(4)])
    for f, r in enumerate(slot_rows):
        gift[f, 0:MOVED] = r[OWN:SLOTS]
        gift[f, MOVED : 2 * MOVED] = r[SLOTS + OWN : 2 * SLOTS]
    pl.semaphore_wait(barrier, n - me)
    gift_copy = swap(gift, given, 8)
    gift_copy.start()
    move_copies = [swap(act_ref.at[:, OWN + i], moved.at[:, i], 2 + i) for i in range(MOVED)]
    for c in move_copies:
        c.start()
    gift_copy.wait()
    rows1 = []
    for f, r in enumerate(slot_rows):
        g = given[f]
        kept = jnp.concatenate([r[0:OWN], r[SLOTS : SLOTS + OWN]], axis=0)
        mixed = jnp.concatenate([r[0:half], g[0:MOVED], r[SLOTS : SLOTS + half], g[MOVED : 2 * MOVED]], axis=0)
        rows1.append(jnp.where(heavy, kept, mixed))
    mine1[...] = packed(rows1)
    share(mine1, got1, send1, recv1)
    def row_ids(slots):
        v = jnp.full((1, 128), -1, jnp.int32)
        for j, slot in enumerate(slots):
            v = jnp.where(lane // 16 == j, jnp.where(slot < count, ids_ref[slot], -1), v)
        return v

    info[0:1] = row_ids(range(OWN))
    info[1:2] = row_ids(list(range(half)) + list(range(OWN, OWN + MOVED)))
    info[2:8] = jnp.full((6, 128), count, jnp.int32)
    info_copy = swap(info, rinfo, 0)
    info_copy.start()
    for c in late:
        c.start()
    for c in early:
        c.wait()
    for i in range(MOVED):
        move_copies[i].wait()

    def choose(i, _):
        for f in range(4):
            v = jnp.where(
                heavy, x[f, half + i].astype(F32).reshape(256, 128), moved[f, i].astype(F32).reshape(256, 128)
            )
            x[f, half + i] = v.astype(BF16).reshape(x.shape[2:])
        return 0

    lax.fori_loop(0, MOVED, choose, 0)

    def sum_of(*refs):
        total = refs[0].astype(F32)
        for r in refs[1:]:
            total = total + r.astype(F32)
        return total.astype(BF16)

    @pl.when(me == 0)
    def _():
        for b in range(3):
            k0, k1, k2 = wn[b, top, first], ws[b, top, second], ws[b, top, first]
            wa[b, top, first] = sum_of(k0, k1, k2)
            wa[b, top, second] = sum_of(k0, k1)
            wda[b, top, first] = sum_of(wd[b, top, first], wd[b, top, second], wd[b, low, second])

    norms(rows1, mine1, got1, send1, recv1, gain1_ref, shift1_ref, per_frame, p1)

    def prep(i, tiles):
        for t in range(2):
            j = 2 * i + t
            rows = slice(16 + t * 272, 272 + t * 272)
            for q in range(4):
                v = x[q, j].astype(F32).reshape(256, 128)
                h = silu_of_half(v * p1[q, 0, pl.ds(j, 1), :] + p1[q, 1, pl.ds(j, 1), :])
                left, right = shifted(h, 16)
                k = (q % 2) * 384
                tiles[q // 2, rows, k : k + 128] = left.astype(BF16)
                tiles[q // 2, rows, k + 128 : k + 256] = h.astype(BF16)
                tiles[q // 2, rows, k + 256 : k + 384] = right.astype(BF16)

    def conv(tiles, terms):
        acc = jnp.zeros((512, 256), F32)
        for p, w in terms:
            for b in range(3):
                r = b * 16
                pair = jnp.concatenate([tiles[p, r : r + 256, :], tiles[p, r + 272 : r + 528, :]], axis=0)
                acc = acc + jnp.dot(pair, w[b], preferred_element_type=F32)
        return acc

    def build(i, z, which, acc, frame):
        col = lax.broadcasted_iota(jnp.int32, (256, 128), 0) % 8
        rows = pl.ds(pl.multiple_of(i * 128, 128), 128)
        for e in range(2):
            for t in range(2):
                v = acc[t * 256 : t * 256 + 256, e * 128 : e * 128 + 128]
                if frame is not None:
                    v = v + x[frame + e, 2 * i + t].astype(F32).reshape(256, 128)
                sf[z, which, e, t * 256 : t * 256 + 256] = v
        for e in range(2):
            even = sf[z, which, e, pl.ds(0, 256, stride=2), :]
            odd = sf[z, which, e, pl.ds(1, 256, stride=2), :]
            prev = jnp.where(col == 0, 0.0, pltpu.roll(odd, 1, axis=0))
            for c, v in enumerate((prev, even, odd)):
                v = v.reshape(2, 8, 2, 8, 128)
                up_rows, low_rows = v[:, :, 0], v[:, :, 1]
                above = jnp.concatenate([jnp.zeros((2, 1, 8, 128), F32), low_rows[:, :7]], axis=1)
                k = e * 384 + c * 128
                for b, u in enumerate((above, up_rows, low_rows)):
                    lhs[which, b, rows, k : k + 128] = u.reshape(128, 128).astype(BF16)

    pairs = OWN // 2

    def part_copy(i):
        return remote(next1.at[i], part1.at[i], psend.at[i], precv.at[i], {"tm": me + 1})

    def step(i, _):
        def onward(pair, z, tiles):
            build(pair, z, 2, conv(tiles, ((1, wn),)), None)
            build(pair, z, 1, conv(tiles, ((1, ws), (0, wn))), 2)

        prep(2 * i + 1, bufo.at[i])
        onward(2 * i, 0, bufe.at[i])
        prep(jnp.minimum(2 * i + 2, pairs - 1), bufe.at[i + 1])
        onward(2 * i + 1, 1, bufo.at[i])
        rows = pl.ds(pl.multiple_of(i * 256, 256), 256)

        @pl.when(me < n)
        def _():
            both = [jnp.concatenate([lhs[1, b, rows, :], lhs[2, b, rows, :]], axis=0) for b in range(3)]
            out = dot(both[0], wd[0]) + dot(both[1], wd[1]) + dot(both[2], wd[2])
            outd[1, rows, :] = out[0:256]
            outd[2, rows, :] = out[256:512]

        next1[i, 0] = (outd[1, rows, second] + outd[2, rows, first]).astype(SENT1)
        next1[i, 1] = outd[2, rows, second].astype(SENT1)

        @pl.when(me < n - 1)
        def _():
            part_copy(i).start()

        return 0

    prep(0, bufe.at[0])
    lax.fori_loop(0, 2, step, 0)

    sums2 = (send2, recv2), (send3, recv3)
    rows2 = []
    for i in range(2):
        rows = slice(i * 256, i * 256 + 256)
        build(2 * i, 0, 0, conv(bufe.at[i], ((0, wa),)), 0)
        build(2 * i + 1, 1, 0, conv(bufo.at[i], ((0, wa),)), 0)

        @pl.when(me < n)
        def _():
            outd[0, rows, :] = (
                dot(lhs[0, 0, rows, :], wda[0]) + dot(lhs[0, 1, rows, :], wda[1]) + dot(lhs[0, 2, rows, :], wda[2])
            )

        @pl.when(me > 0)
        def _():
            part_copy(i).wait_recv()

        totals = []
        for f in range(2):
            v = outd[0, rows, f * 128 : f * 128 + 128]
            if f == 1:
                v = v + outd[1, rows, first]
            v = (v + part1[i, f].astype(F32)).astype(BF16)
            level[rows, f * 128 : f * 128 + 128] = v
            v = v.astype(F32).reshape(HALF, 64, 128)
            totals.append(jnp.concatenate([jnp.sum(v, axis=1), jnp.sum(v * v, axis=1)], axis=0))
        rows2.append(grouped_sums(totals))
        mine2[i] = packed(rows2[i])
        share(mine2.at[i], got2.at[i], *sums2[i])
    for c in late:
        c.wait()
    for i in range(2):
        rows = slice(i * 256, i * 256 + 256)
        planes[rows, :] = dot(plane[...], level[rows, :]).astype(BF16)

    @pl.when(me == 0)
    def _():
        conv2a[0] = sum_of(conv2[0], conv2[1], conv2[2])
        conv2a[1] = sum_of(conv2[0], conv2[1])
        for i in range(9):
            down2a[i] = sum_of(down2[0, i], down2[1, i], down2[2, i])

    row = lax.broadcasted_iota(jnp.int32, (128, 128), 0)

    def back_y(v, row):
        return jnp.where(row % 16 < 4, 0.0, pltpu.roll(v, 4, axis=0))

    def back_x(v, row):
        return jnp.where(row % 4 < 1, 0.0, pltpu.roll(v, 1, axis=0))

    def on_y(v, row):
        return jnp.where(row % 16 >= 12, 0.0, pltpu.roll(v, v.shape[0] - 4, axis=0))

    def on_x(v, row):
        return jnp.where(row % 4 >= 3, 0.0, pltpu.roll(v, v.shape[0] - 1, axis=0))

    def second_hidden(h):
        norms(rows2[h], mine2.at[h], got2.at[h], *sums2[h], gain2_ref, shift2_ref, per_frame / 4, p2.at[h])
        here = row[0:64]
        for f in range(2):
            scale = p2[h, f, 0].reshape(HALF, 1, 128)
            bias = p2[h, f, 1].reshape(HALF, 1, 128)
            for yp in range(2):
                for xp in range(2):
                    q = yp * 2 + xp
                    r = h * 256 + q * 64
                    v = planes[r : r + 64, f * 128 : f * 128 + 128].astype(F32)
                    v = silu_of_half(v.reshape(HALF, 16, 128) * scale + bias).reshape(64, 128)
                    vy = (back_y if yp else on_y)(v, here)
                    move_x = back_x if xp else on_x
                    for k, u in enumerate((v, move_x(v, here), vy, move_x(vy, here))):
                        blocks[f, q * 4 + k, h * 64 : h * 64 + 64] = u.astype(BF16)

    taps = (((1, 1), (0, 0), (1, 0)), ((0, 0), (1, 0), (0, 1)))

    def gathered(f, h):
        rows = []
        for yp in range(2):
            for xp in range(2):
                cells = []
                for b in range(3):
                    for c in range(3):
                        (py, sy), (px, sx) = taps[yp][b], taps[xp][c]
                        cells.append(blocks[f, (py * 2 + px) * 4 + sy * 2 + sx, h * 64 : h * 64 + 64])
                rows.append(jnp.concatenate(cells, axis=1))
        return jnp.concatenate(rows, axis=0)

    def wide(*parts):
        return jnp.concatenate(parts, axis=1)

    def tall(*parts):
        return jnp.concatenate(parts, axis=0)

    row2 = lax.broadcasted_iota(jnp.int32, (64, 256), 0)

    def spread(which, acc, h):
        u = [acc[q * 64 : q * 64 + 64] for q in range(4)]
        u1x, u3x, u2y, u3y = back_x(u[1], row2), back_x(u[3], row2), back_y(u[2], row2), back_y(u[3], row2)
        u3yx = back_x(u3y, row2)
        for i, v in enumerate((u3yx, u2y, u3y, u1x, u[0], u[1], u3x, u[2], u[3])):
            ublocks[which, i, h * 64 : h * 64 + 64] = v.astype(BF16)

    def onward2(h):
        spread(3, dot(gathered(1, h), conv2[0]), h)
        spread(2, dot(wide(gathered(0, h), gathered(1, h)), tall(conv2[0], conv2[1])), h)

    def own2(h):
        levels = planes[h * 256 : h * 256 + 256]
        both = wide(gathered(0, h), gathered(1, h), levels[:, second])
        spread(1, dot(both, tall(conv2a[1], conv2[2], short[...])), h)
        spread(0, dot(wide(gathered(0, h), levels[:, first]), tall(conv2a[0], short[...])), h)

    second_hidden(0)
    onward2(0)
    own2(0)
    second_hidden(1)
    onward2(1)

    def down_sum(terms):
        acc = jnp.zeros((128, 256), F32)
        for which, w in terms:
            for i in range(9):
                acc = acc + dot(ublocks[which, i], w[i])
        return acc

    skip_copy = remote(next2.at[1], part2.at[1], sems.at[12], sems.at[13], {"tm": me + 2})
    next_copy = remote(next2.at[0], part2.at[0], sems.at[14], sems.at[15], {"tm": me + 1})

    @pl.when(me < n - 2)
    def _():
        next2[1] = down_sum(((2, down2.at[0]), (3, down2.at[1]))).astype(SENT2)
        skip_copy.start()

    own2(1)

    @pl.when(me < n - 1)
    def _():
        next2[0] = down_sum(((0, down2.at[0]), (1, down2.at[1]), (2, down2.at[2]))).astype(SENT2)
        next_copy.start()

    own = down_sum(((0, down2a),))
    info_copy.wait()
    low_lane = lane < half * 16
    its_heavy = rinfo[2:3, :] == cap
    my_ids = jnp.where(low_lane | heavy, info[0:1, :], rinfo[1:2, :])
    its_ids = jnp.where(low_lane | its_heavy, rinfo[0:1, :], info[1:2, :])
    wanted = lax.axis_index("tile") * OWN + row // 16
    cell = row % 16 == lax.broadcasted_iota(jnp.int32, (128, 128), 1) % 16
    mine = jnp.where((wanted == my_ids) & cell, 1.0, 0.0).astype(BF16)
    its = jnp.where((wanted == its_ids) & cell, 1.0, 0.0).astype(BF16)

    @pl.when(me > 1)
    def _():
        skip_copy.wait_recv()

    @pl.when(me > 0)
    def _():
        next_copy.wait_recv()

    enc[...] = (own + part2[1].astype(F32) + part2[0].astype(F32)).astype(BF16)
    enc_copy = swap(enc, renc, 1)
    enc_copy.start()
    kept = dot(mine, enc[...])
    shared(mine1, got1, send1, recv1)
    for i in range(2):
        shared(mine2.at[i], got2.at[i], *sums2[i])

    @pl.when(me < n - 1)
    def _():
        for i in range(2):
            part_copy(i).wait_send()
        next_copy.wait_send()

    @pl.when(me < n - 2)
    def _():
        skip_copy.wait_send()

    enc_copy.wait()
    out_ref[...] = (kept + dot(its, renc[...])).astype(BF16).reshape(out_ref.shape)


def encode(acts, ids, counts, params, n):
    (
        first_gain,
        first_shift,
        first_conv,
        first_down,
        second_gain,
        second_shift,
        second_conv,
        second_short,
        second_down,
    ) = params
    cells = acts.shape[2:]
    rows = OWN * 64
    vm = pltpu.VMEM
    line = lambda v: v.reshape(1, 128)
    return pl.pallas_call(
        functools.partial(main_kernel, n, float(cells[0] * cells[1] * (cells[2] // GROUPS))),
        out_shape=jax.ShapeDtypeStruct((OWN * 4, 4, 256), BF16),
        in_specs=[ANY, SMEM, SMEM, VMEM, VMEM, ANY, ANY, VMEM, VMEM, ANY, ANY, ANY, ANY],
        out_specs=VMEM,
        scratch_shapes=[
            vm((4, SLOTS) + cells, BF16),
            vm((4, MOVED) + cells, BF16),
            vm((4, 2 * MOVED, 128), F32),
            vm((4, 2 * MOVED, 128), F32),
            vm((8, 128), jnp.int32),
            vm((8, 128), jnp.int32),
            vm((4, 2 * SLOTS, 128), F32),
            vm((3, 1152, 256), BF16),
            vm((2, 1152, 256), BF16),
            vm((128, 256), BF16),
            vm((3, 9, 256, 256), BF16),
            vm((9, 256, 256), BF16),
            vm((HALF * 64, HALF * 64), BF16),
            vm((4, 128), F32),
            vm((n, 4, 128), F32),
            vm((2, 2, 128), F32),
            vm((2, n, 2, 128), F32),
            vm((4, 2, OWN, 128), F32),
            vm((2, 2, 2, HALF, 128), F32),
            vm((3, 2, 560, 768), BF16),
            vm((2, 2, 560, 768), BF16),
            vm((3, 768, 256), BF16),
            vm((3, 768, 256), BF16),
            vm((3, 768, 256), BF16),
            vm((3, 768, 256), BF16),
            vm((3, 768, 256), BF16),
            vm((2, 3, 2, 512, 128), F32),
            vm((3, 3, rows, 768), BF16),
            vm((3, rows, 256), F32),
            vm((2, 2, 256, 128), SENT1),
            vm((2, 2, 256, 128), SENT1),
            vm((rows, 256), BF16),
            vm((rows, 256), BF16),
            vm((2, 16, 128, 128), BF16),
            vm((4, 9, 128, 256), BF16),
            vm((2, OWN * 16, 256), SENT2),
            vm((2, OWN * 16, 256), SENT2),
            vm((OWN * 16, 256), BF16),
            vm((OWN * 16, 256), BF16),
            pltpu.SemaphoreType.DMA((n,)),
            pltpu.SemaphoreType.DMA((n,)),
            pltpu.SemaphoreType.DMA((n,)),
            pltpu.SemaphoreType.DMA((n,)),
            pltpu.SemaphoreType.DMA((n,)),
            pltpu.SemaphoreType.DMA((n,)),
            pltpu.SemaphoreType.DMA((2,)),
            pltpu.SemaphoreType.DMA((2,)),
            pltpu.SemaphoreType.DMA((18,)),
            pltpu.SemaphoreType.DMA((25,)),
        ],
        name="encode",
        compiler_params=pltpu.CompilerParams(collective_id=0, has_side_effects=True, vmem_limit_bytes=LIMIT),
    )(
        acts,
        ids,
        counts,
        line(first_gain),
        line(first_shift),
        first_conv.reshape(3, 3, 384, 128),
        first_down.reshape(3, 3, 384, 128),
        line(second_gain),
        line(second_shift),
        second_conv.reshape(3, 1152, 256),
        second_short,
        second_down.reshape(3, 9, 256, 256),
        jnp.asarray(plane_matrix(), BF16),
    )


def body(activations, tile_ids, tile_counts, *params):
    n = lax.axis_size("tm")
    latents = encode(activations, tile_ids, tile_counts, params, n)
    return latents.reshape(1, OWN, 4, 4, 256)


def solution(mesh):
    placed = (
        P(("groups", "tm"), "tile", None, None, None),
        P(("groups", "tile")),
        P(("groups", "tile")),
    ) + (P(),) * 9
    return jax.shard_map(
        body,
        mesh=mesh,
        in_specs=placed,
        out_specs=P(("groups", "tm"), "tile", None, None, None),
        check_vma=False,
    )
```

```python
import functools

import jax
import jax.numpy as jnp
import numpy as np
from jax import lax
from jax.experimental import pallas as pl
from jax.experimental.pallas import tpu as pltpu
from jax.sharding import PartitionSpec as P

GROUPS = 32
OWN = 8
MOVED = 4
SLOTS = OWN + MOVED
HALF = OWN // 2
EPS = 1e-06
F32 = jnp.float32
BF16 = jnp.bfloat16
SENT1 = jnp.bfloat16
SENT2 = jnp.bfloat16
MESH = pl.DeviceIdType.MESH
VMEM = pl.BlockSpec(memory_space=pltpu.VMEM)
SMEM = pl.BlockSpec(memory_space=pltpu.SMEM)
ANY = pl.BlockSpec(memory_space=pl.ANY)
LIMIT = 56 << 20


def silu_of_half(w):
    return w + w * jnp.tanh(w)


def dot(a, b):
    return jnp.dot(a, b, preferred_element_type=F32)


def shifted(v, side):
    rows = v.shape[0]
    col = lax.broadcasted_iota(jnp.int32, v.shape, 0) % side
    left = jnp.where(col == 0, 0.0, pltpu.roll(v, 1, axis=0))
    right = jnp.where(col == side - 1, 0.0, pltpu.roll(v, rows - 1, axis=0))
    return left, right


def plane_matrix():
    m = np.zeros((2, 2, HALF, 4, 4, HALF, 8, 8), np.float32)
    for yp in range(2):
        for xp in range(2):
            for t in range(HALF):
                for y in range(4):
                    for x in range(4):
                        m[yp, xp, t, y, x, t, 2 * y + yp, 2 * x + xp] = 1.0
    return m.reshape(HALF * 64, HALF * 64)


def main_kernel(
    n,
    per_frame,
    act_ref,
    ids_ref,
    count_ref,
    gain1_ref,
    shift1_ref,
    conv1_hbm,
    down1_hbm,
    gain2_ref,
    shift2_ref,
    conv2_hbm,
    short_hbm,
    down2_hbm,
    plane_hbm,
    out_ref,
    x,
    moved,
    gift,
    given,
    info,
    rinfo,
    s_ref,
    conv2,
    conv2a,
    short,
    down2,
    down2a,
    plane,
    mine1,
    got1,
    mine2,
    got2,
    p1,
    p2,
    bufe,
    bufo,
    ws,
    wn,
    wa,
    wd,
    wda,
    sf,
    lhs,
    outd,
    next1,
    part1,
    level,
    planes,
    blocks,
    ublocks,
    next2,
    part2,
    enc,
    renc,
    send1,
    recv1,
    send2,
    recv2,
    send3,
    recv3,
    psend,
    precv,
    sems,
    local,
):
    me = lax.axis_index("tm")
    partner = 1 - lax.axis_index("tile")
    cap = act_ref.shape[1]
    barrier = pltpu.get_barrier_semaphore()
    pl.semaphore_signal(barrier, inc=1, device_id={"tile": partner}, device_id_type=MESH)

    def greet(k, _):
        pl.semaphore_signal(barrier, inc=1, device_id={"tm": k}, device_id_type=MESH)
        return 0

    lax.fori_loop(0, me, greet, 0)

    used = [0]

    def copy_in(src, dst):
        c = pltpu.make_async_copy(src, dst, local.at[used[0]])
        used[0] += 1
        return c

    half = OWN - MOVED
    fetch = [
        copy_in(act_ref.at[:, 0:half], x.at[:, 0:half]),
        copy_in(act_ref.at[:, half:OWN], x.at[:, half:OWN]),
        copy_in(act_ref.at[:, OWN : OWN + MOVED], x.at[:, OWN : OWN + MOVED]),
    ]
    for c in fetch:
        c.start()
    lane = lax.broadcasted_iota(jnp.int32, (1, 128), 1)
    count = count_ref[0]
    heavy = jnp.full((1, 128), count, jnp.int32) == cap

    def remote(src, dst, send_sem, recv_sem, target):
        return pltpu.make_async_remote_copy(
            src_ref=src, dst_ref=dst, send_sem=send_sem, recv_sem=recv_sem, device_id=target, device_id_type=MESH
        )

    def swap(src, dst, i):
        return remote(src, dst, sems.at[2 * i], sems.at[2 * i + 1], {"tile": partner})

    def quarter(rows):
        return lax.broadcasted_iota(jnp.int32, (rows, 128), 1) % 4

    def grouped_sums(sums):
        ri = lax.broadcasted_iota(jnp.int32, (128, 128), 0) // (128 // GROUPS)
        ci = lax.broadcasted_iota(jnp.int32, (128, 128), 1) // (128 // GROUPS)
        same = jnp.where(ri == ci, 1.0, 0.0).astype(F32)
        rows = jnp.dot(
            jnp.concatenate(sums, axis=0), same, precision=lax.Precision.HIGHEST, preferred_element_type=F32
        )
        size = sums[0].shape[0]
        return [rows[f * size : (f + 1) * size] for f in range(len(sums))]

    def packed(rows):
        total = rows[0]
        for r in rows[1:]:
            total = total + r
        k = total.shape[0] // 4
        v = total[0:k]
        for q in range(1, 4):
            v = jnp.where(quarter(k) == q, total[k * q : k * q + k], v)
        return v

    def unpacked(v):
        at = quarter(v.shape[0])
        parts = [jnp.where(at == 0, v, 0.0)]
        for q in range(1, 4):
            parts.append(pltpu.roll(jnp.where(at == q, v, 0.0), 128 - q, axis=1))
        w = jnp.concatenate(parts, axis=0)
        w = w + pltpu.roll(w, 1, axis=1)
        return w + pltpu.roll(w, 2, axis=1)

    top, low = slice(0, 384), slice(384, 768)
    first, second = slice(0, 128), slice(128, 256)

    def sum_copy(mine, got, sent, here, k):
        return remote(mine, got.at[k], sent.at[k], here.at[k], {"tm": me + k})

    def share(mine, got, sent, here):
        def start(i, _):
            sum_copy(mine, got, sent, here, n - me - i).start()
            return 0

        lax.fori_loop(1, n - me, start, 0)

    def shared(mine, got, sent, here):
        def wait(k, _):
            sum_copy(mine, got, sent, here, k).wait_send()
            return 0

        lax.fori_loop(1, n - me, wait, 0)

    def norms(rows, mine, got, sent, here, gain, shift, size, out):
        def take(k, run):
            sum_copy(mine, got, sent, here, k).wait_recv()
            return run + got[k]

        run = unpacked(lax.fori_loop(1, me + 1, take, jnp.zeros(mine.shape, F32)))
        tiles = rows[0].shape[0] // 2
        start = (me * len(rows)).astype(F32)
        for i, r in enumerate(rows):
            run = run + r
            inv_count = jnp.full((1, 128), 1.0, F32) / (jnp.zeros((1, 128), F32) + (start + float(i + 1)) * size)
            m = run[0:tiles] * inv_count
            var = run[tiles : 2 * tiles] * inv_count - m * m
            scale = lax.rsqrt(jnp.maximum(var, 0.0) + EPS) * gain[...]
            out[i, 0] = 0.5 * scale
            out[i, 1] = 0.5 * (shift[...] - m * scale)

    zero = jnp.zeros((384, 128), BF16)
    for b in range(3):
        ws[b, 384:768, 0:128] = zero
        wa[b, 384:768, 0:128] = zero
        wn[b, 0:384, 128:256] = zero
        wd[b, 384:768, 0:128] = zero
        wda[b, 384:768, 0:128] = zero
    edge = jnp.zeros((16, 768), BF16)
    for tiles in (bufe, bufo):
        for i in range(2):
            for p in range(2):
                for r in (0, 272, 544):
                    tiles[i, p, r : r + 16] = edge


    @pl.when(me == 0)
    def _():
        part1[...] = jnp.zeros_like(part1)
        part2[...] = jnp.zeros_like(part2)

    @pl.when(me == 1)
    def _():
        part2[1] = jnp.zeros_like(part2[1])

    early = [
        copy_in(h.at[a], w.at[:, r, c])
        for h, a, w, r, c in (
            (conv1_hbm, 0, wn, top, first),
            (conv1_hbm, 1, wn, low, first),
            (conv1_hbm, 0, wn, low, second),
            (conv1_hbm, 2, ws, top, first),
            (conv1_hbm, 1, ws, top, second),
            (conv1_hbm, 2, ws, low, second),
            (conv1_hbm, 2, wa, top, first),
            (conv1_hbm, 1, wa, top, second),
            (conv1_hbm, 2, wa, low, second),
            (down1_hbm, 2, wd, top, first),
            (down1_hbm, 0, wd, top, second),
            (down1_hbm, 1, wd, low, second),
            (down1_hbm, 2, wda, top, first),
            (down1_hbm, 0, wda, top, second),
            (down1_hbm, 1, wda, low, second),
        )
    ]
    late = [
        copy_in(a, b)
        for a, b in (
            (plane_hbm, plane),
            (conv2_hbm, conv2),
            (conv2_hbm.at[2], conv2a.at[0]),
            (conv2_hbm.at[1], conv2a.at[1]),
            (short_hbm, short),
            (down2_hbm, down2),
            (down2_hbm.at[2], down2a),
        )
    ]

    def add_up(f, j, v):
        s_ref[f, pl.ds(j, 1), :] = jnp.sum(v, axis=0, keepdims=True)
        s_ref[f, pl.ds(SLOTS + j, 1), :] = jnp.sum(v * v, axis=0, keepdims=True)

    def count_slot(j, _):
        for f in range(4):
            add_up(f, j, x[f, j].astype(F32).reshape(256, 128))
        return 0

    fetch[0].wait()
    lax.fori_loop(0, half, count_slot, 0)
    fetch[1].wait()
    fetch[2].wait()
    for c in early:
        c.start()
    lax.fori_loop(half, SLOTS, count_slot, 0)
    slot_rows = grouped_sums([s_ref[f] for f in range(4)])
    for f, r in enumerate(slot_rows):
        gift[f, 0:MOVED] = r[OWN:SLOTS]
        gift[f, MOVED : 2 * MOVED] = r[SLOTS + OWN : 2 * SLOTS]
    pl.semaphore_wait(barrier, n - me)
    gift_copy = swap(gift, given, 8)
    gift_copy.start()
    move_copies = [swap(act_ref.at[:, OWN + i], moved.at[:, i], 2 + i) for i in range(MOVED)]
    for c in move_copies:
        c.start()
    gift_copy.wait()
    rows1 = []
    for f, r in enumerate(slot_rows):
        g = given[f]
        kept = jnp.concatenate([r[0:OWN], r[SLOTS : SLOTS + OWN]], axis=0)
        mixed = jnp.concatenate([r[0:half], g[0:MOVED], r[SLOTS : SLOTS + half], g[MOVED : 2 * MOVED]], axis=0)
        rows1.append(jnp.where(heavy, kept, mixed))
    mine1[...] = packed(rows1)
    share(mine1, got1, send1, recv1)
    def row_ids(slots):
        v = jnp.full((1, 128), -1, jnp.int32)
        for j, slot in enumerate(slots):
            v = jnp.where(lane // 16 == j, jnp.where(slot < count, ids_ref[slot], -1), v)
        return v

    info[0:1] = row_ids(range(OWN))
    info[1:2] = row_ids(list(range(half)) + list(range(OWN, OWN + MOVED)))
    info[2:8] = jnp.full((6, 128), count, jnp.int32)
    info_copy = swap(info, rinfo, 0)
    info_copy.start()
    for c in late:
        c.start()
    for c in early:
        c.wait()
    for i in range(MOVED):
        move_copies[i].wait()

    def choose(i, _):
        for f in range(4):
            v = jnp.where(
                heavy, x[f, half + i].astype(F32).reshape(256, 128), moved[f, i].astype(F32).reshape(256, 128)
            )
            x[f, half + i] = v.astype(BF16).reshape(x.shape[2:])
        return 0

    lax.fori_loop(0, MOVED, choose, 0)

    def sum_of(*refs):
        total = refs[0].astype(F32)
        for r in refs[1:]:
            total = total + r.astype(F32)
        return total.astype(BF16)

    @pl.when(me == 0)
    def _():
        for b in range(3):
            k0, k1, k2 = wn[b, top, first], ws[b, top, second], ws[b, top, first]
            wa[b, top, first] = sum_of(k0, k1, k2)
            wa[b, top, second] = sum_of(k0, k1)
            wda[b, top, first] = sum_of(wd[b, top, first], wd[b, top, second], wd[b, low, second])

    norms(rows1, mine1, got1, send1, recv1, gain1_ref, shift1_ref, per_frame, p1)

    def prep(i, tiles):
        for t in range(2):
            j = 2 * i + t
            rows = slice(16 + t * 272, 272 + t * 272)
            for q in range(4):
                v = x[q, j].astype(F32).reshape(256, 128)
                h = silu_of_half(v * p1[q, 0, pl.ds(j, 1), :] + p1[q, 1, pl.ds(j, 1), :])
                left, right = shifted(h, 16)
                k = (q % 2) * 384
                tiles[q // 2, rows, k : k + 128] = left.astype(BF16)
                tiles[q // 2, rows, k + 128 : k + 256] = h.astype(BF16)
                tiles[q // 2, rows, k + 256 : k + 384] = right.astype(BF16)

    def conv(tiles, terms):
        acc = jnp.zeros((512, 256), F32)
        for p, w in terms:
            for b in range(3):
                r = b * 16
                pair = jnp.concatenate([tiles[p, r : r + 256, :], tiles[p, r + 272 : r + 528, :]], axis=0)
                acc = acc + jnp.dot(pair, w[b], preferred_element_type=F32)
        return acc

    def build(i, z, which, acc, frame):
        col = lax.broadcasted_iota(jnp.int32, (256, 128), 0) % 8
        rows = pl.ds(pl.multiple_of(i * 128, 128), 128)
        for e in range(2):
            for t in range(2):
                v = acc[t * 256 : t * 256 + 256, e * 128 : e * 128 + 128]
                if frame is not None:
                    v = v + x[frame + e, 2 * i + t].astype(F32).reshape(256, 128)
                sf[z, which, e, t * 256 : t * 256 + 256] = v
        for e in range(2):
            even = sf[z, which, e, pl.ds(0, 256, stride=2), :]
            odd = sf[z, which, e, pl.ds(1, 256, stride=2), :]
            prev = jnp.where(col == 0, 0.0, pltpu.roll(odd, 1, axis=0))
            for c, v in enumerate((prev, even, odd)):
                v = v.reshape(2, 8, 2, 8, 128)
                up_rows, low_rows = v[:, :, 0], v[:, :, 1]
                above = jnp.concatenate([jnp.zeros((2, 1, 8, 128), F32), low_rows[:, :7]], axis=1)
                k = e * 384 + c * 128
                for b, u in enumerate((above, up_rows, low_rows)):
                    lhs[which, b, rows, k : k + 128] = u.reshape(128, 128).astype(BF16)

    pairs = OWN // 2

    def part_copy(i):
        return remote(next1.at[i], part1.at[i], psend.at[i], precv.at[i], {"tm": me + 1})

    def step(i, _):
        def onward(pair, z, tiles):
            build(pair, z, 2, conv(tiles, ((1, wn),)), None)
            build(pair, z, 1, conv(tiles, ((1, ws), (0, wn))), 2)

        prep(2 * i + 1, bufo.at[i])
        onward(2 * i, 0, bufe.at[i])
        prep(jnp.minimum(2 * i + 2, pairs - 1), bufe.at[i + 1])
        onward(2 * i + 1, 1, bufo.at[i])
        rows = pl.ds(pl.multiple_of(i * 256, 256), 256)

        @pl.when(me < n)
        def _():
            both = [jnp.concatenate([lhs[1, b, rows, :], lhs[2, b, rows, :]], axis=0) for b in range(3)]
            out = dot(both[0], wd[0]) + dot(both[1], wd[1]) + dot(both[2], wd[2])
            outd[1, rows, :] = out[0:256]
            outd[2, rows, :] = out[256:512]

        next1[i, 0] = (outd[1, rows, second] + outd[2, rows, first]).astype(SENT1)
        next1[i, 1] = outd[2, rows, second].astype(SENT1)

        @pl.when(me < n - 1)
        def _():
            part_copy(i).start()

        return 0

    prep(0, bufe.at[0])
    lax.fori_loop(0, 2, step, 0)

    sums2 = (send2, recv2), (send3, recv3)
    rows2 = []
    for i in range(2):
        rows = slice(i * 256, i * 256 + 256)
        build(2 * i, 0, 0, conv(bufe.at[i], ((0, wa),)), 0)
        build(2 * i + 1, 1, 0, conv(bufo.at[i], ((0, wa),)), 0)

        @pl.when(me < n)
        def _():
            outd[0, rows, :] = (
                dot(lhs[0, 0, rows, :], wda[0]) + dot(lhs[0, 1, rows, :], wda[1]) + dot(lhs[0, 2, rows, :], wda[2])
            )

        @pl.when(me > 0)
        def _():
            part_copy(i).wait_recv()

        totals = []
        for f in range(2):
            v = outd[0, rows, f * 128 : f * 128 + 128]
            if f == 1:
                v = v + outd[1, rows, first]
            v = (v + part1[i, f].astype(F32)).astype(BF16)
            level[rows, f * 128 : f * 128 + 128] = v
            v = v.astype(F32).reshape(HALF, 64, 128)
            totals.append(jnp.concatenate([jnp.sum(v, axis=1), jnp.sum(v * v, axis=1)], axis=0))
        rows2.append(grouped_sums(totals))
        mine2[i] = packed(rows2[i])
        share(mine2.at[i], got2.at[i], *sums2[i])
    for c in late:
        c.wait()
    for i in range(2):
        rows = slice(i * 256, i * 256 + 256)
        planes[rows, :] = dot(plane[...], level[rows, :]).astype(BF16)

    @pl.when(me == 0)
    def _():
        conv2a[0] = sum_of(conv2[0], conv2[1], conv2[2])
        conv2a[1] = sum_of(conv2[0], conv2[1])
        for i in range(9):
            down2a[i] = sum_of(down2[0, i], down2[1, i], down2[2, i])

    row = lax.broadcasted_iota(jnp.int32, (128, 128), 0)

    def back_y(v, row):
        return jnp.where(row % 16 < 4, 0.0, pltpu.roll(v, 4, axis=0))

    def back_x(v, row):
        return jnp.where(row % 4 < 1, 0.0, pltpu.roll(v, 1, axis=0))

    def on_y(v, row):
        return jnp.where(row % 16 >= 12, 0.0, pltpu.roll(v, v.shape[0] - 4, axis=0))

    def on_x(v, row):
        return jnp.where(row % 4 >= 3, 0.0, pltpu.roll(v, v.shape[0] - 1, axis=0))

    def second_hidden(h):
        norms(rows2[h], mine2.at[h], got2.at[h], *sums2[h], gain2_ref, shift2_ref, per_frame / 4, p2.at[h])
        here = row[0:64]
        for f in range(2):
            scale = p2[h, f, 0].reshape(HALF, 1, 128)
            bias = p2[h, f, 1].reshape(HALF, 1, 128)
            for yp in range(2):
                for xp in range(2):
                    q = yp * 2 + xp
                    r = h * 256 + q * 64
                    v = planes[r : r + 64, f * 128 : f * 128 + 128].astype(F32)
                    v = silu_of_half(v.reshape(HALF, 16, 128) * scale + bias).reshape(64, 128)
                    vy = (back_y if yp else on_y)(v, here)
                    move_x = back_x if xp else on_x
                    for k, u in enumerate((v, move_x(v, here), vy, move_x(vy, here))):
                        blocks[f, q * 4 + k, h * 64 : h * 64 + 64] = u.astype(BF16)

    taps = (((1, 1), (0, 0), (1, 0)), ((0, 0), (1, 0), (0, 1)))

    def gathered(f, h):
        rows = []
        for yp in range(2):
            for xp in range(2):
                cells = []
                for b in range(3):
                    for c in range(3):
                        (py, sy), (px, sx) = taps[yp][b], taps[xp][c]
                        cells.append(blocks[f, (py * 2 + px) * 4 + sy * 2 + sx, h * 64 : h * 64 + 64])
                rows.append(jnp.concatenate(cells, axis=1))
        return jnp.concatenate(rows, axis=0)

    def wide(*parts):
        return jnp.concatenate(parts, axis=1)

    def tall(*parts):
        return jnp.concatenate(parts, axis=0)

    row2 = lax.broadcasted_iota(jnp.int32, (64, 256), 0)

    def spread(which, acc, h):
        u = [acc[q * 64 : q * 64 + 64] for q in range(4)]
        u1x, u3x, u2y, u3y = back_x(u[1], row2), back_x(u[3], row2), back_y(u[2], row2), back_y(u[3], row2)
        u3yx = back_x(u3y, row2)
        for i, v in enumerate((u3yx, u2y, u3y, u1x, u[0], u[1], u3x, u[2], u[3])):
            ublocks[which, i, h * 64 : h * 64 + 64] = v.astype(BF16)

    def onward2(h):
        spread(3, dot(gathered(1, h), conv2[0]), h)
        spread(2, dot(wide(gathered(0, h), gathered(1, h)), tall(conv2[0], conv2[1])), h)

    def own2(h):
        levels = planes[h * 256 : h * 256 + 256]
        both = wide(gathered(0, h), gathered(1, h), levels[:, second])
        spread(1, dot(both, tall(conv2a[1], conv2[2], short[...])), h)
        spread(0, dot(wide(gathered(0, h), levels[:, first]), tall(conv2a[0], short[...])), h)

    second_hidden(0)
    onward2(0)
    own2(0)
    second_hidden(1)
    onward2(1)

    def down_sum(terms):
        acc = jnp.zeros((128, 256), F32)
        for which, w in terms:
            for i in range(9):
                acc = acc + dot(ublocks[which, i], w[i])
        return acc

    skip_copy = remote(next2.at[1], part2.at[1], sems.at[12], sems.at[13], {"tm": me + 2})
    next_copy = remote(next2.at[0], part2.at[0], sems.at[14], sems.at[15], {"tm": me + 1})

    @pl.when(me < n - 2)
    def _():
        next2[1] = down_sum(((2, down2.at[0]), (3, down2.at[1]))).astype(SENT2)
        skip_copy.start()

    own2(1)

    @pl.when(me < n - 1)
    def _():
        next2[0] = down_sum(((0, down2.at[0]), (1, down2.at[1]), (2, down2.at[2]))).astype(SENT2)
        next_copy.start()

    own = down_sum(((0, down2a),))
    info_copy.wait()
    low_lane = lane < half * 16
    its_heavy = rinfo[2:3, :] == cap
    my_ids = jnp.where(low_lane | heavy, info[0:1, :], rinfo[1:2, :])
    its_ids = jnp.where(low_lane | its_heavy, rinfo[0:1, :], info[1:2, :])
    wanted = lax.axis_index("tile") * OWN + row // 16
    cell = row % 16 == lax.broadcasted_iota(jnp.int32, (128, 128), 1) % 16
    mine = jnp.where((wanted == my_ids) & cell, 1.0, 0.0).astype(BF16)
    its = jnp.where((wanted == its_ids) & cell, 1.0, 0.0).astype(BF16)

    @pl.when(me > 1)
    def _():
        skip_copy.wait_recv()

    @pl.when(me > 0)
    def _():
        next_copy.wait_recv()

    enc[...] = (own + part2[1].astype(F32) + part2[0].astype(F32)).astype(BF16)
    enc_copy = swap(enc, renc, 1)
    enc_copy.start()
    kept = dot(mine, enc[...])
    shared(mine1, got1, send1, recv1)
    for i in range(2):
        shared(mine2.at[i], got2.at[i], *sums2[i])

    @pl.when(me < n - 1)
    def _():
        for i in range(2):
            part_copy(i).wait_send()
        next_copy.wait_send()

    @pl.when(me < n - 2)
    def _():
        skip_copy.wait_send()

    enc_copy.wait()
    out_ref[...] = (kept + dot(its, renc[...])).astype(BF16).reshape(out_ref.shape)


def encode(acts, ids, counts, params, n):
    (
        first_gain,
        first_shift,
        first_conv,
        first_down,
        second_gain,
        second_shift,
        second_conv,
        second_short,
        second_down,
    ) = params
    cells = acts.shape[2:]
    rows = OWN * 64
    vm = pltpu.VMEM
    line = lambda v: v.reshape(1, 128)
    return pl.pallas_call(
        functools.partial(main_kernel, n, float(cells[0] * cells[1] * (cells[2] // GROUPS))),
        out_shape=jax.ShapeDtypeStruct((OWN * 4, 4, 256), BF16),
        in_specs=[ANY, SMEM, SMEM, VMEM, VMEM, ANY, ANY, VMEM, VMEM, ANY, ANY, ANY, ANY],
        out_specs=VMEM,
        scratch_shapes=[
            vm((4, SLOTS) + cells, BF16),
            vm((4, MOVED) + cells, BF16),
            vm((4, 2 * MOVED, 128), F32),
            vm((4, 2 * MOVED, 128), F32),
            vm((8, 128), jnp.int32),
            vm((8, 128), jnp.int32),
            vm((4, 2 * SLOTS, 128), F32),
            vm((3, 1152, 256), BF16),
            vm((2, 1152, 256), BF16),
            vm((128, 256), BF16),
            vm((3, 9, 256, 256), BF16),
            vm((9, 256, 256), BF16),
            vm((HALF * 64, HALF * 64), BF16),
            vm((4, 128), F32),
            vm((n, 4, 128), F32),
            vm((2, 2, 128), F32),
            vm((2, n, 2, 128), F32),
            vm((4, 2, OWN, 128), F32),
            vm((2, 2, 2, HALF, 128), F32),
            vm((3, 2, 560, 768), BF16),
            vm((2, 2, 560, 768), BF16),
            vm((3, 768, 256), BF16),
            vm((3, 768, 256), BF16),
            vm((3, 768, 256), BF16),
            vm((3, 768, 256), BF16),
            vm((3, 768, 256), BF16),
            vm((2, 3, 2, 512, 128), F32),
            vm((3, 3, rows, 768), BF16),
            vm((3, rows, 256), F32),
            vm((2, 2, 256, 128), SENT1),
            vm((2, 2, 256, 128), SENT1),
            vm((rows, 256), BF16),
            vm((rows, 256), BF16),
            vm((2, 16, 128, 128), BF16),
            vm((4, 9, 128, 256), BF16),
            vm((2, OWN * 16, 256), SENT2),
            vm((2, OWN * 16, 256), SENT2),
            vm((OWN * 16, 256), BF16),
            vm((OWN * 16, 256), BF16),
            pltpu.SemaphoreType.DMA((n,)),
            pltpu.SemaphoreType.DMA((n,)),
            pltpu.SemaphoreType.DMA((n,)),
            pltpu.SemaphoreType.DMA((n,)),
            pltpu.SemaphoreType.DMA((n,)),
            pltpu.SemaphoreType.DMA((n,)),
            pltpu.SemaphoreType.DMA((2,)),
            pltpu.SemaphoreType.DMA((2,)),
            pltpu.SemaphoreType.DMA((18,)),
            pltpu.SemaphoreType.DMA((25,)),
        ],
        name="encode",
        compiler_params=pltpu.CompilerParams(collective_id=0, has_side_effects=True, vmem_limit_bytes=LIMIT),
    )(
        acts,
        ids,
        counts,
        line(first_gain),
        line(first_shift),
        first_conv.reshape(3, 3, 384, 128),
        first_down.reshape(3, 3, 384, 128),
        line(second_gain),
        line(second_shift),
        second_conv.reshape(3, 1152, 256),
        second_short,
        second_down.reshape(3, 9, 256, 256),
        jnp.asarray(plane_matrix(), BF16),
    )


def body(activations, tile_ids, tile_counts, *params):
    n = lax.axis_size("tm")
    latents = encode(activations, tile_ids, tile_counts, params, n)
    return latents.reshape(1, OWN, 4, 4, 256)


def solution(mesh):
    placed = (
        P(("groups", "tm"), "tile", None, None, None),
        P(("groups", "tile")),
        P(("groups", "tile")),
    ) + (P(),) * 9
    return jax.shard_map(
        body,
        mesh=mesh,
        in_specs=placed,
        out_specs=P(("groups", "tm"), "tile", None, None, None),
        check_vma=False,
    )
```
